512 devices in a mesh: space: 64 (over z, x, y_lo), sta: 8 (over y_hi, core).
Axes of the slice: x: 4, y: 8 (y_hi: 4, y_lo: 2; y = y_hi * 2 + y_lo), z: 8, core: 2. Of those that a mesh axis runs over, the one named last changes fastest.
Arguments:
- coarse_times: float32 [16, 320, 32, 128], P('sta', 'space'), as said below
- model_map: int32 [320, 32, 128], P('space'), may hold values from 0 to 63
- slowness: float32 [64], replicated, may hold values from 0.12 to 0.3
- picks: float32 [256, 16], replicated
- pick_mask: int32 [256, 16], replicated, may hold values from 0 to 1, as said below
Outputs:
- refined: float32 [16, 320, 32, 128], P(None, 'space', 'sta')
- density: float32 [256, 320, 32, 128], P(None, 'space', 'sta')
The draws below stay inside these ranges and needn't reach their ends.
Inputs may be any that keep to these rules, and one draw needn't show every extreme that they name: `pick_mask`: each event has at least 4 stations with a pick. `coarse_times`: zero at each station's own cell and positive elsewhere.
All inputs are finite; a program needn't handle non-finite values.
Results may differ from the reference program's by a relative error of at most 0.0003.
Values sent between devices are 32-bit elements; how exact they have to be, the bound alone decides.
A program may use at most 64 MiB of HBM per device.

```python
import math
import jax
import jax.numpy as jnp
from jax import lax

NY = 32
NZ = 128
ROUNDS = 12
STATIONS = 16
MODELS = 64
EVENTS = 256
NX = 320


def station_spots(key):
    base = jax.random.fold_in(key, 11)
    key_x, key_y = jax.random.split(base)
    spot_x = jax.random.randint(key_x, (STATIONS,), 0, NX)
    spot_y = jax.random.randint(key_y, (STATIONS,), 0, NY)
    return (spot_x, spot_y)


def draw_coarse_times(key, part):
    spot_x, spot_y = station_spots(key)
    grid_x = jnp.arange(NX, dtype=jnp.float32)[None, :, None, None]
    grid_y = jnp.arange(NY, dtype=jnp.float32)[None, None, :, None]
    grid_z = jnp.arange(NZ, dtype=jnp.float32)[None, None, None, :]
    delta_x = grid_x - spot_x.astype(jnp.float32)[:, None, None, None]
    delta_y = grid_y - spot_y.astype(jnp.float32)[:, None, None, None]
    spread = jnp.sqrt(delta_x * delta_x + delta_y * delta_y + grid_z * grid_z)
    factor = jax.random.uniform(jax.random.fold_in(key, 23), (STATIONS, NX, NY, NZ), jnp.float32, 1.05, 1.35)
    return 0.2 * spread * factor


def draw_picks(key, part):
    spot_x, spot_y = station_spots(key)
    keys = jax.random.split(jax.random.fold_in(key, 31), 5)
    hypo_x = jax.random.uniform(keys[0], (EVENTS, 1), jnp.float32, 0.0, NX - 1.0)
    hypo_y = jax.random.uniform(keys[1], (EVENTS, 1), jnp.float32, 0.0, NY - 1.0)
    hypo_z = jax.random.uniform(keys[2], (EVENTS, 1), jnp.float32, 0.0, NZ - 1.0)
    anchor = jax.random.uniform(keys[3], (EVENTS, 1), jnp.float32, 0.0, 2.0)
    delta_x = hypo_x - spot_x.astype(jnp.float32)[None, :]
    delta_y = hypo_y - spot_y.astype(jnp.float32)[None, :]
    spread = jnp.sqrt(delta_x * delta_x + delta_y * delta_y + hypo_z * hypo_z)
    noise = 0.1 * jax.random.normal(keys[4], (EVENTS, STATIONS), jnp.float32)
    return 0.2 * spread + anchor + noise


def draw_pick_mask(key, part):
    base = jax.random.fold_in(key, 41)
    keys = jax.random.split(base, EVENTS)
    orders = jax.vmap(lambda single: jax.random.permutation(single, STATIONS))(keys)
    ranks = jnp.argsort(orders, axis=1)
    picked = jax.random.randint(jax.random.fold_in(key, 43), (EVENTS, 1), 4, STATIONS + 1)
    return (ranks < picked).astype(jnp.int32)


def with_ends(array, own_key, low, top_value):
    dims = array.shape
    index_at = [jax.random.randint(jax.random.fold_in(own_key, axis), (), 0, dims[axis]) for axis in range(len(dims))]
    array = array.at[tuple(index_at)].set(low)
    longest = dims.index(max(dims))
    index_at[longest] = (index_at[longest] + 1) % dims[longest]
    return array.at[tuple(index_at)].set(top_value)


def setup_inputs(seed: int = 0) -> dict:
    streams_of = jax.random.split(jax.random.key(seed), 6)
    return {
        "coarse_times": draw_coarse_times(jax.random.fold_in(streams_of[5], 71), 0),
        "model_map": with_ends(jax.random.randint(streams_of[1], (NX, NY, NZ), 0, MODELS), jax.random.fold_in(streams_of[1], 1), 0, MODELS - 1).astype(jnp.int32),
        "slowness": jnp.clip(jnp.exp(jax.random.uniform(streams_of[2], (MODELS,), jnp.float32, math.log(0.12), math.log(0.3))), 0.12, 0.3),
        "picks": draw_picks(jax.random.fold_in(streams_of[5], 71), 0),
        "pick_mask": draw_pick_mask(jax.random.fold_in(streams_of[5], 71), 0),
    }


BIG = 1000000.0
pick_sigma = 0.25
grid_step = 1.0

def godunov(near_one, near_two, near_three, speed):
    lowest = jnp.minimum(jnp.minimum(near_one, near_two), near_three)
    highest = jnp.maximum(jnp.maximum(near_one, near_two), near_three)
    middle = jnp.maximum(jnp.minimum(near_one, near_two), jnp.minimum(jnp.maximum(near_one, near_two), near_three))
    gap_mid = middle - lowest
    gap_high = highest - lowest
    two_sided = 0.5 * (gap_mid + jnp.sqrt(jnp.maximum(2.0 * speed * speed - gap_mid * gap_mid, 0.0)))
    gap_sum = gap_mid + gap_high
    squares = gap_mid * gap_mid + gap_high * gap_high - speed * speed
    three_sided = (gap_sum + jnp.sqrt(jnp.maximum(gap_sum * gap_sum - 3.0 * squares, 0.0))) / 3.0
    increase = jnp.where(speed <= gap_mid, speed, jnp.where(two_sided <= gap_high, two_sided, three_sided))
    return lowest + increase

def sweep_one(table, speed):
    padded = jnp.pad(table, 1, constant_values=BIG)
    along_x = jnp.minimum(padded[:-2, 1:-1, 1:-1], padded[2:, 1:-1, 1:-1])
    along_y = jnp.minimum(padded[1:-1, :-2, 1:-1], padded[1:-1, 2:, 1:-1])
    along_z = jnp.minimum(padded[1:-1, 1:-1, :-2], padded[1:-1, 1:-1, 2:])
    return jnp.minimum(table, godunov(along_x, along_y, along_z, speed))

def misfit_block(event_pair, flat_tables):
    arrivals, observed = event_pair
    pick_count = lax.optimization_barrier(jnp.sum(observed, 1))
    residual = arrivals[:, :, None] - flat_tables[None]
    anchor_shift = lax.optimization_barrier(jnp.sum(observed[:, :, None] * residual, 1)) / pick_count[:, None]
    deviation = residual - anchor_shift[:, None, :]
    return lax.optimization_barrier(jnp.sum(observed[:, :, None] * deviation * deviation, 1))

def density_block(event_pair, flat_tables):
    misfit = misfit_block(event_pair, flat_tables)
    score = -0.5 * misfit / (pick_sigma * pick_sigma)
    top_score = lax.optimization_barrier(jnp.max(score, 1))
    cell_weights = jnp.exp(score - top_score[:, None])
    mass_sum = lax.optimization_barrier(jnp.sum(cell_weights, 1))
    return cell_weights / mass_sum[:, None]

def reference(coarse_times, model_map, slowness, picks, pick_mask):
    speed = grid_step * slowness[model_map]
    tables = coarse_times
    for round_index in range(ROUNDS):
        tables = lax.map(lambda table: sweep_one(table, speed), tables)
    flat_tables = tables.reshape(STATIONS, -1)
    observed = pick_mask.astype(jnp.float32)
    blocks = lax.map(lambda event_pair: density_block(event_pair, flat_tables), (picks.reshape(-1, 4, STATIONS), observed.reshape(-1, 4, STATIONS)))
    density = blocks.reshape(EVENTS, NX, NY, NZ)
    return (tables, density)
```

```python
import jax
import jax.numpy as jnp
from jax import lax
from jax.experimental import pallas as pl
from jax.experimental.pallas import tpu as pltpu
from jax.sharding import PartitionSpec as P

ROUNDS = 12

BIG = 1000000.0
pick_sigma = 0.25
grid_step = 1.0
block_events = 32
NEAR = 2


def merge_softmax_stats(top, mass, slots, count):
    best = top
    for k in range(count):
        best = jnp.maximum(best, slots[k, 0:2])
    total = mass * jnp.exp(top - best)
    for k in range(count):
        total = total + slots[k, 2:4] * jnp.exp(slots[k, 0:2] - best)
    return best, total


def stats_kernel(local_ref, out_ref, first, second, mid, send_sem, recv_sem):
    space = lax.axis_index("space")
    sta = lax.axis_index("sta")
    stas = lax.axis_size("sta")
    lines = lax.axis_size("space") // NEAR
    line = space // NEAR
    member = (space % NEAR) * stas + sta
    members = NEAR * stas

    def member_id(k):
        other = (member + k) % members
        return {"space": line * NEAR + other // stas, "sta": other % stas}

    def line_id(k):
        other = (line + k) % lines
        return {"space": other * NEAR + space % NEAR, "sta": sta}

    barrier = pltpu.get_barrier_semaphore()

    def greet(ids, count):
        def one(k, carry):
            pl.semaphore_signal(barrier, inc=1, device_id=ids(k), device_id_type=pl.DeviceIdType.MESH)
            return carry

        lax.fori_loop(1, count, one, 0)

    greet(member_id, members)
    greet(line_id, lines)
    pl.semaphore_wait(barrier, members + lines - 2)

    def exchange(src, slots, ids, count, phase):
        def copy(k):
            return pltpu.make_async_remote_copy(
                src_ref=src,
                dst_ref=slots.at[k - 1],
                send_sem=send_sem.at[phase, k - 1],
                recv_sem=recv_sem.at[phase, k - 1],
                device_id=ids(k),
                device_id_type=pl.DeviceIdType.MESH,
            )

        def start(k, carry):
            copy(k).start()
            return carry

        def wait(k, carry):
            copy(k).wait()
            return carry

        lax.fori_loop(1, count, start, 0)
        lax.fori_loop(1, count, wait, 0)

    exchange(local_ref, first, member_id, members, 0)
    top, mass = merge_softmax_stats(local_ref[0:2], local_ref[2:4], first, members - 1)
    mid[0:2] = top
    mid[2:4] = mass
    exchange(mid, second, line_id, lines, 1)
    top, mass = merge_softmax_stats(top, mass, second, lines - 1)
    out_ref[0:2] = top
    out_ref[2:4] = mass


def global_stats(top, mass):
    events = top.shape[0]
    local = jnp.concatenate([top.reshape(2, -1), mass.reshape(2, -1)], 0)
    members = NEAR * lax.axis_size("sta")
    lines = lax.axis_size("space") // NEAR
    longest = max(members, lines)
    out = pl.pallas_call(
        stats_kernel,
        out_shape=jax.ShapeDtypeStruct(local.shape, jnp.float32),
        in_specs=[pl.BlockSpec(memory_space=pltpu.VMEM)],
        out_specs=pl.BlockSpec(memory_space=pltpu.VMEM),
        scratch_shapes=[
            pltpu.VMEM((members - 1,) + local.shape, jnp.float32),
            pltpu.VMEM((lines - 1,) + local.shape, jnp.float32),
            pltpu.VMEM(local.shape, jnp.float32),
            pltpu.SemaphoreType.DMA((2, longest)),
            pltpu.SemaphoreType.DMA((2, longest)),
        ],
        compiler_params=pltpu.CompilerParams(collective_id=0, has_side_effects=True),
        name="stats",
    )(local)
    return out[0:2].reshape(events), out[2:4].reshape(events)


def extended_2(block, sides, width):
    for axis, dim in sides:
        count = lax.axis_size(axis)
        forward = [(i, i + 1) for i in range(count - 1)]
        backward = [(target, source) for source, target in forward]
        low = lax.ppermute(
            lax.slice_in_dim(block, block.shape[dim] - width, None, axis=dim), axis, forward
        )
        high = lax.ppermute(lax.slice_in_dim(block, 0, width, axis=dim), axis, backward)
        block = jnp.concatenate([low, block, high], axis=dim)
    return block


def godunov(near_one, near_two, near_three, speed):
    lowest = jnp.minimum(jnp.minimum(near_one, near_two), near_three)
    highest = jnp.maximum(jnp.maximum(near_one, near_two), near_three)
    middle = jnp.maximum(
        jnp.minimum(near_one, near_two), jnp.minimum(jnp.maximum(near_one, near_two), near_three)
    )
    gap_mid = middle - lowest
    gap_high = highest - lowest
    two_sided = 0.5 * (
        gap_mid + jnp.sqrt(jnp.maximum(2.0 * speed * speed - gap_mid * gap_mid, 0.0))
    )
    gap_sum = gap_mid + gap_high
    squares = gap_mid * gap_mid + gap_high * gap_high - speed * speed
    three_sided = (gap_sum + jnp.sqrt(jnp.maximum(gap_sum * gap_sum - 3.0 * squares, 0.0))) / 3.0
    increase = jnp.where(
        speed <= gap_mid, speed, jnp.where(two_sided <= gap_high, two_sided, three_sided)
    )
    return lowest + increase


def relax(extended, speed):
    centre = extended[:, 1:-1]
    along_x = jnp.minimum(extended[:, :-2], extended[:, 2:])
    padded = jnp.pad(centre, ((0, 0), (0, 0), (1, 1), (1, 1)), constant_values=BIG)
    along_y = jnp.minimum(padded[:, :, :-2, 1:-1], padded[:, :, 2:, 1:-1])
    along_z = jnp.minimum(padded[:, :, 1:-1, :-2], padded[:, :, 1:-1, 2:])
    return jnp.minimum(centre, godunov(along_x, along_y, along_z, speed[None]))


def close_rims(extended, rim_width, at_lower, at_upper):
    cell_count = extended.shape[1]
    position = lax.broadcasted_iota(jnp.int32, (1, cell_count, 1, 1), 1)
    outside = (position < rim_width) & at_lower | (position >= cell_count - rim_width) & at_upper
    return jnp.where(outside, BIG, extended)


def misfit_block(event_pair, flat_tables):
    arrivals, observed = event_pair
    pick_count = jnp.sum(observed, 1)
    residual = arrivals[:, :, None] - flat_tables[None]
    anchor_shift = jnp.sum(observed[:, :, None] * residual, 1) / pick_count[:, None]
    deviation = residual - anchor_shift[:, None, :]
    return jnp.sum(observed[:, :, None] * deviation * deviation, 1)


def body(coarse_times, model_map, slowness, picks, pick_mask):
    levels = lax.broadcasted_iota(jnp.int32, (slowness.shape[0], 1, 1, 1), 0)
    speed = grid_step * jnp.sum(
        jnp.where(model_map[None] == levels, slowness[:, None, None, None], 0.0), 0
    )
    position_space = lax.axis_index("space")
    devices_space = lax.axis_size("space")
    at_lower = position_space == 0
    at_upper = position_space == devices_space - 1
    tables = coarse_times

    def one_round(round_index, tables):
        extended = extended_2(tables, (("space", 1),), 1)
        return relax(close_rims(extended, 1, at_lower, at_upper), speed)

    tables = lax.fori_loop(0, ROUNDS, one_round, tables)
    refined = lax.all_to_all(tables, "sta", split_axis=2, concat_axis=0, tiled=True)
    stations = refined.shape[0]
    flat_tables = refined.reshape(stations, -1)
    observed = pick_mask.astype(jnp.float32)
    blocks = lax.map(
        lambda event_pair: misfit_block(event_pair, flat_tables),
        (picks.reshape(-1, block_events, stations), observed.reshape(-1, block_events, stations)),
    )
    score = -0.5 * blocks.reshape(picks.shape[0], -1) / (pick_sigma * pick_sigma)
    local_top = jnp.max(score, 1)
    cell_weights = jnp.exp(score - local_top[:, None])
    top_score, mass_sum = global_stats(local_top, jnp.sum(cell_weights, 1))
    scale = jnp.exp(local_top - top_score) / mass_sum
    density = cell_weights * scale[:, None]
    density = density.reshape(picks.shape[0], refined.shape[1], refined.shape[2], refined.shape[3])
    return (refined, density)


def solution(mesh):
    placed = (P("sta", "space", None, None), P("space", None, None), P(), P(), P())
    return jax.shard_map(
        body,
        mesh=mesh,
        in_specs=placed,
        out_specs=(P(None, "space", "sta", None), P(None, "space", "sta", None)),
        check_vma=False,
    )
```

```python
import jax
import jax.numpy as jnp
from jax import lax
from jax.experimental import pallas as pl
from jax.experimental.pallas import tpu as pltpu
from jax.sharding import PartitionSpec as P

ROUNDS = 12

BIG = 1000000.0
pick_sigma = 0.25
grid_step = 1.0
block_events = 32
NEAR = 2


def merge_softmax_stats(top, mass, slots, count):
    best = top
    for k in range(count):
        best = jnp.maximum(best, slots[k, 0:2])
    total = mass * jnp.exp(top - best)
    for k in range(count):
        total = total + slots[k, 2:4] * jnp.exp(slots[k, 0:2] - best)
    return best, total


def stats_kernel(local_ref, out_ref, first, second, mid, send_sem, recv_sem):
    space = lax.axis_index("space")
    sta = lax.axis_index("sta")
    stas = lax.axis_size("sta")
    lines = lax.axis_size("space") // NEAR
    line = space // NEAR
    member = (space % NEAR) * stas + sta
    members = NEAR * stas

    def member_id(k):
        other = (member + k) % members
        return {"space": line * NEAR + other // stas, "sta": other % stas}

    def line_id(k):
        other = (line + k) % lines
        return {"space": other * NEAR + space % NEAR, "sta": sta}

    barrier = pltpu.get_barrier_semaphore()

    def greet(ids, count):
        def one(k, carry):
            pl.semaphore_signal(barrier, inc=1, device_id=ids(k), device_id_type=pl.DeviceIdType.MESH)
            return carry

        lax.fori_loop(1, count, one, 0)

    greet(member_id, members)
    greet(line_id, lines)
    pl.semaphore_wait(barrier, members + lines - 2)

    def exchange(src, slots, ids, count, phase):
        def copy(k):
            return pltpu.make_async_remote_copy(
                src_ref=src,
                dst_ref=slots.at[k - 1],
                send_sem=send_sem.at[phase, k - 1],
                recv_sem=recv_sem.at[phase, k - 1],
                device_id=ids(k),
                device_id_type=pl.DeviceIdType.MESH,
            )

        def start(k, carry):
            copy(k).start()
            return carry

        def wait(k, carry):
            copy(k).wait()
            return carry

        lax.fori_loop(1, count, start, 0)
        lax.fori_loop(1, count, wait, 0)

    exchange(local_ref, first, member_id, members, 0)
    top, mass = merge_softmax_stats(local_ref[0:2], local_ref[2:4], first, members - 1)
    mid[0:2] = top
    mid[2:4] = mass
    exchange(mid, second, line_id, lines, 1)
    top, mass = merge_softmax_stats(top, mass, second, lines - 1)
    out_ref[0:2] = top
    out_ref[2:4] = mass


def global_stats(top, mass):
    events = top.shape[0]
    local = jnp.concatenate([top.reshape(2, -1), mass.reshape(2, -1)], 0)
    members = NEAR * lax.axis_size("sta")
    lines = lax.axis_size("space") // NEAR
    longest = max(members, lines)
    out = pl.pallas_call(
        stats_kernel,
        out_shape=jax.ShapeDtypeStruct(local.shape, jnp.float32),
        in_specs=[pl.BlockSpec(memory_space=pltpu.VMEM)],
        out_specs=pl.BlockSpec(memory_space=pltpu.VMEM),
        scratch_shapes=[
            pltpu.VMEM((members - 1,) + local.shape, jnp.float32),
            pltpu.VMEM((lines - 1,) + local.shape, jnp.float32),
            pltpu.VMEM(local.shape, jnp.float32),
            pltpu.SemaphoreType.DMA((2, longest)),
            pltpu.SemaphoreType.DMA((2, longest)),
        ],
        compiler_params=pltpu.CompilerParams(collective_id=0, has_side_effects=True),
        name="stats",
    )(local)
    return out[0:2].reshape(events), out[2:4].reshape(events)


HALO = 4
PAD = 8


def speed_kernel(table_ref, map_ref, out_ref):
    for plane in range(map_ref.shape[0]):
        index = map_ref[plane]
        table = jnp.broadcast_to(table_ref[...], index.shape)
        out_ref[plane] = grid_step * jnp.take_along_axis(table, index, axis=1)


def speed_of(model_map, slowness):
    lanes = model_map.shape[-1]
    table = jnp.pad(slowness, (0, lanes - slowness.shape[0])).reshape(1, lanes)
    return pl.pallas_call(
        speed_kernel,
        out_shape=jax.ShapeDtypeStruct(model_map.shape, jnp.float32),
        in_specs=[pl.BlockSpec(memory_space=pltpu.VMEM)] * 2,
        out_specs=pl.BlockSpec(memory_space=pltpu.VMEM),
        name="speed",
    )(table, model_map)


def godunov(near_one, near_two, near_three, speed):
    small = jnp.minimum(near_one, near_two)
    large = jnp.maximum(near_one, near_two)
    lowest = jnp.minimum(small, near_three)
    highest = jnp.maximum(large, near_three)
    middle = jnp.maximum(small, jnp.minimum(large, near_three))
    gap_mid = middle - lowest
    gap_high = highest - lowest
    spread = highest - middle
    square = speed * speed
    mid_square = gap_mid * gap_mid
    reach = gap_high * gap_high + spread * spread
    two = square <= reach
    inner = jnp.where(two, 2.0 * square, 3.0 * square - reach) - mid_square
    root = jnp.sqrt(jnp.maximum(inner, 0.0))
    base = gap_mid + jnp.where(two, 0.0, gap_high)
    steep = (base + root) * jnp.where(two, 0.5, 1.0 / 3.0)
    return lowest + jnp.where(speed <= gap_mid, speed, steep)


def travel_kernel(
    times_ref,
    speed_ref,
    refined_ref,
    tab,
    spd,
    swap_in,
    swap_speed,
    halo_in,
    halo_speed,
    edge_out,
    stage,
    arrived,
    start_send,
    start_recv,
    halo_send,
    halo_recv,
    all_send,
    all_recv,
):
    space = lax.axis_index("space")
    sta = lax.axis_index("sta")
    stas = lax.axis_size("sta")
    lines = lax.axis_size("space") // NEAR
    line = space // NEAR
    half = space % NEAR
    depth, rows, lanes = speed_ref.shape
    own = NEAR * depth
    count = own + 2 * HALO
    piece = stage.shape[2]
    member = half * stas + sta
    members = NEAR * stas
    station = NEAR * sta + half
    inside = pl.ds(PAD, rows)
    mesh_id = pl.DeviceIdType.MESH

    def at(other_line, other_half):
        return {"space": ((other_line + lines) % lines) * NEAR + other_half, "sta": sta}

    def member_at(other):
        return {"space": line * NEAR + other // stas, "sta": other % stas}

    barrier = pltpu.get_barrier_semaphore()

    def greet(j, carry):
        pl.semaphore_signal(
            barrier, inc=1, device_id=member_at((member + j) % members), device_id_type=mesh_id
        )
        return carry

    for other_line in (line - 1, line + 1):
        for other_half in range(NEAR):
            pl.semaphore_signal(
                barrier, inc=1, device_id=at(other_line, other_half), device_id_type=mesh_id
            )
    lax.fori_loop(1, members, greet, 0)

    rim = jnp.full((PAD, lanes), BIG, jnp.float32)

    def rims(plane, carry):
        for side in range(2):
            tab[side, plane, pl.ds(0, PAD)] = rim
            tab[side, plane, pl.ds(PAD + rows, PAD)] = rim
        return carry

    lax.fori_loop(0, count, rims, 0)
    pl.semaphore_wait(barrier, members - 1 + 2 * NEAR)

    away = line + 2 * half - 1
    first = half * (depth - HALO)

    def start_copy(j):
        if j == 0:
            src, dst, who = times_ref.at[1 - half], swap_in, at(line, 1 - half)
        elif j == 1:
            src, dst, who = speed_ref, swap_speed, at(line, 1 - half)
        elif j < 4:
            src = times_ref.at[j - 2, pl.ds(first, HALO)]
            dst, who = halo_in.at[0, 1 - half], at(away, j - 2)
        else:
            src = speed_ref.at[pl.ds(first, HALO)]
            dst, who = halo_speed.at[1 - half], at(away, j - 4)
        slot = j if j < 2 else (2 if j < 4 else 4) + (1 - half)
        return pltpu.make_async_remote_copy(
            src_ref=src,
            dst_ref=dst,
            send_sem=start_send.at[j],
            recv_sem=start_recv.at[slot],
            device_id=who,
            device_id_type=mesh_id,
        )

    def start_arrival(slot):
        if slot == 0:
            src, dst = times_ref.at[1 - half], swap_in
        elif slot == 1:
            src, dst = speed_ref, swap_speed
        elif slot < 4:
            src, dst = times_ref.at[0, pl.ds(0, HALO)], halo_in.at[0, slot - 2]
        else:
            src, dst = speed_ref.at[pl.ds(0, HALO)], halo_speed.at[slot - 4]
        return pltpu.make_async_remote_copy(
            src_ref=src,
            dst_ref=dst,
            send_sem=start_send.at[slot],
            recv_sem=start_recv.at[slot],
            device_id=at(line, 1 - half),
            device_id_type=mesh_id,
        )

    for j in (2, 3, 0, 4, 5, 1):
        start_copy(j).start()

    at_lower = line == 0
    at_upper = line == lines - 1

    for i in range(depth):
        tab[0, HALO + half * depth + i, inside] = times_ref[half, i]
        spd[HALO + half * depth + i] = speed_ref[i]
    for slot in range(6):
        start_arrival(slot).wait_recv()
    for i in range(depth):
        tab[0, HALO + (1 - half) * depth + i, inside] = swap_in[i]
        spd[HALO + (1 - half) * depth + i] = swap_speed[i]
    for i in range(HALO):
        spd[i] = halo_speed[0, i]
        spd[HALO + own + i] = halo_speed[1, i]

    def place_halo(exchange, side):
        for i in range(HALO):
            tab[side, i, inside] = jnp.where(at_lower, BIG, halo_in[exchange, 0, i])
            tab[side, HALO + own + i, inside] = jnp.where(at_upper, BIG, halo_in[exchange, 1, i])

    place_halo(0, 0)

    lane = lax.broadcasted_iota(jnp.int32, (rows, lanes), 1)

    def plane_value(side, plane):
        centre = tab[side, plane, inside]
        along_x = jnp.minimum(tab[side, plane - 1, inside], tab[side, plane + 1, inside])
        along_y = jnp.minimum(
            tab[side, plane, pl.ds(PAD - 1, rows)], tab[side, plane, pl.ds(PAD + 1, rows)]
        )
        before = jnp.where(lane == 0, BIG, pltpu.roll(centre, 1, 1))
        after = jnp.where(lane == lanes - 1, BIG, pltpu.roll(centre, lanes - 1, 1))
        along_z = jnp.minimum(before, after)
        value = jnp.minimum(centre, godunov(along_x, along_y, along_z, spd[plane]))
        outside = (at_lower & (plane < HALO)) | (at_upper & (plane >= HALO + own))
        return jnp.maximum(value, jnp.where(outside, BIG, -BIG))

    def sweep(side, total, plane_at, store):
        def one(j, carry):
            plane = plane_at(j)
            store(plane, plane_value(side, plane))
            return carry

        lax.fori_loop(0, total, one, 0)

    def into(side):
        def store(plane, value):
            tab[side, plane, inside] = value

        return store

    def into_stage(plane, value):
        place = plane - HALO
        for j in range(stas):
            stage[(place // depth) * stas + j, place % depth] = value[piece * j : piece * (j + 1)]

    def into_edge(side, exchange, lower):
        def store(plane, value):
            tab[side, plane, inside] = value
            edge_out[exchange, 0 if lower else 1, plane - (HALO if lower else own)] = value

        return store

    def halo_copy(exchange, lower):
        slot = 1 if lower else 0
        return pltpu.make_async_remote_copy(
            src_ref=edge_out.at[exchange - 1, 0 if lower else 1],
            dst_ref=halo_in.at[exchange, slot],
            send_sem=halo_send.at[exchange - 1, slot],
            recv_sem=halo_recv.at[exchange - 1, slot],
            device_id=at(line - 1 if lower else line + 1, half),
            device_id_type=mesh_id,
        )

    def last_round(side, exchange):
        sweep(side, HALO, lambda j: HALO + j, into_edge(1 - side, exchange - 1, True))
        halo_copy(exchange, True).start()
        sweep(side, HALO, lambda j: own + j, into_edge(1 - side, exchange - 1, False))
        halo_copy(exchange, False).start()
        sweep(side, own - 2 * HALO, lambda j: 2 * HALO + j, into(1 - side))

    exchanges = ROUNDS // HALO
    side = 0
    for exchange in range(exchanges):
        final = exchange == exchanges - 1
        if exchange == 0:
            for r in range(HALO - 1):
                sweep(side, count - 2 - 2 * r, lambda j, r=r: r + 1 + j, into(1 - side))
                side = 1 - side
        else:
            start = side
            for r in range(HALO - 1):
                sweep(side, own - 2 - 2 * r, lambda j, r=r: HALO + 1 + r + j, into(1 - side))
                side = 1 - side
            for lower in (True, False):
                halo_copy(exchange, lower).wait()
            side = start
            place_halo(exchange, side)
            for r in range(HALO - 1):
                sweep(
                    side,
                    2 * HALO,
                    lambda j, r=r: jnp.where(j < HALO, r + 1 + j, own - 1 - r + j),
                    into(1 - side),
                )
                side = 1 - side
        if final:
            sweep(side, own, lambda j: HALO + j, into_stage)
        else:
            last_round(side, exchange + 1)
            side = 1 - side

    def block_copy(j):
        other = (member + j) % members
        return pltpu.make_async_remote_copy(
            src_ref=stage.at[other],
            dst_ref=arrived.at[station],
            send_sem=all_send.at[j],
            recv_sem=all_recv.at[station],
            device_id=member_at(other),
            device_id_type=mesh_id,
        )

    def block_arrival(j):
        other = (member + j) % members
        source = NEAR * (other % stas) + other // stas
        return pltpu.make_async_remote_copy(
            src_ref=stage.at[other],
            dst_ref=arrived.at[source],
            send_sem=all_send.at[j],
            recv_sem=all_recv.at[source],
            device_id=member_at(other),
            device_id_type=mesh_id,
        )

    def start_block(j, carry):
        block_copy(j).start()
        return carry

    def end_block(j, carry):
        block_copy(j).wait_send()
        block_arrival(j).wait_recv()
        return carry

    lax.fori_loop(1, members, start_block, 0)
    arrived[station] = stage[member]
    for j in range(6):
        start_copy(j).wait_send()
    lax.fori_loop(1, members, end_block, 0)
    refined_ref[...] = arrived[...]


def refined_tables(coarse_times, speed):
    per_device, depth, rows, lanes = coarse_times.shape
    stas = lax.axis_size("sta")
    stations = per_device * stas
    assert per_device == NEAR and ROUNDS % HALO == 0 and HALO <= depth
    piece = rows // stas
    own = NEAR * depth
    count = own + 2 * HALO
    exchanges = ROUNDS // HALO
    plane = (rows, lanes)
    vmem = pl.BlockSpec(memory_space=pltpu.VMEM)
    dma = pltpu.SemaphoreType.DMA
    return pl.pallas_call(
        travel_kernel,
        out_shape=jax.ShapeDtypeStruct((stations, depth, piece, lanes), jnp.float32),
        in_specs=[vmem, vmem],
        out_specs=vmem,
        scratch_shapes=[
            pltpu.VMEM((2, count, rows + 2 * PAD, lanes), jnp.float32),
            pltpu.VMEM((count,) + plane, jnp.float32),
            pltpu.VMEM((depth,) + plane, jnp.float32),
            pltpu.VMEM((depth,) + plane, jnp.float32),
            pltpu.VMEM((exchanges, 2, HALO) + plane, jnp.float32),
            pltpu.VMEM((2, HALO) + plane, jnp.float32),
            pltpu.VMEM((exchanges - 1, 2, HALO) + plane, jnp.float32),
            pltpu.VMEM((NEAR * stas, depth, piece, lanes), jnp.float32),
            pltpu.VMEM((stations, depth, piece, lanes), jnp.float32),
            dma((6,)),
            dma((6,)),
            dma((exchanges - 1, 2)),
            dma((exchanges - 1, 2)),
            dma((NEAR * stas,)),
            dma((stations,)),
        ],
        compiler_params=pltpu.CompilerParams(collective_id=1, has_side_effects=True),
        name="travel",
    )(coarse_times, speed)


def misfit_block(event_pair, flat_tables):
    arrivals, observed = event_pair
    pick_count = jnp.sum(observed, 1)
    residual = arrivals[:, :, None] - flat_tables[None]
    anchor_shift = jnp.sum(observed[:, :, None] * residual, 1) / pick_count[:, None]
    deviation = residual - anchor_shift[:, None, :]
    return jnp.sum(observed[:, :, None] * deviation * deviation, 1)


def body(coarse_times, model_map, slowness, picks, pick_mask):
    refined = refined_tables(coarse_times, speed_of(model_map, slowness))
    stations = refined.shape[0]
    flat_tables = refined.reshape(stations, -1)
    observed = pick_mask.astype(jnp.float32)
    blocks = lax.map(
        lambda event_pair: misfit_block(event_pair, flat_tables),
        (picks.reshape(-1, block_events, stations), observed.reshape(-1, block_events, stations)),
    )
    score = -0.5 * blocks.reshape(picks.shape[0], -1) / (pick_sigma * pick_sigma)
    local_top = jnp.max(score, 1)
    cell_weights = jnp.exp(score - local_top[:, None])
    top_score, mass_sum = global_stats(local_top, jnp.sum(cell_weights, 1))
    scale = jnp.exp(local_top - top_score) / mass_sum
    density = cell_weights * scale[:, None]
    density = density.reshape(picks.shape[0], refined.shape[1], refined.shape[2], refined.shape[3])
    return (refined, density)


def solution(mesh):
    placed = (P("sta", "space", None, None), P("space", None, None), P(), P(), P())
    return jax.shard_map(
        body,
        mesh=mesh,
        in_specs=placed,
        out_specs=(P(None, "space", "sta", None), P(None, "space", "sta", None)),
        check_vma=False,
    )
```

```python
import jax
import jax.numpy as jnp
from jax import lax
from jax.experimental import pallas as pl
from jax.experimental.pallas import tpu as pltpu
from jax.sharding import PartitionSpec as P

ROUNDS = 12

BIG = 1000000.0
pick_sigma = 0.25
grid_step = 1.0
NEAR = 2


HALO = 4
PAD = 8


def speed_kernel(table_ref, map_ref, out_ref):
    for plane in range(map_ref.shape[0]):
        index = map_ref[plane]
        table = jnp.broadcast_to(table_ref[...], index.shape)
        out_ref[plane] = grid_step * jnp.take_along_axis(table, index, axis=1)


def speed_of(model_map, slowness):
    lanes = model_map.shape[-1]
    table = jnp.pad(slowness, (0, lanes - slowness.shape[0])).reshape(1, lanes)
    return pl.pallas_call(
        speed_kernel,
        out_shape=jax.ShapeDtypeStruct(model_map.shape, jnp.float32),
        in_specs=[pl.BlockSpec(memory_space=pltpu.VMEM)] * 2,
        out_specs=pl.BlockSpec(memory_space=pltpu.VMEM),
        name="speed",
    )(table, model_map)


def godunov(near_one, near_two, near_three, speed):
    small = jnp.minimum(near_one, near_two)
    large = jnp.maximum(near_one, near_two)
    lowest = jnp.minimum(small, near_three)
    highest = jnp.maximum(large, near_three)
    middle = jnp.maximum(small, jnp.minimum(large, near_three))
    gap_mid = middle - lowest
    gap_high = highest - lowest
    spread = highest - middle
    square = speed * speed
    mid_square = gap_mid * gap_mid
    reach = gap_high * gap_high + spread * spread
    two = square <= reach
    inner = jnp.where(two, 2.0 * square, 3.0 * square - reach) - mid_square
    root = jnp.sqrt(jnp.maximum(inner, 0.0))
    base = gap_mid + jnp.where(two, 0.0, gap_high)
    steep = (base + root) * jnp.where(two, 0.5, 1.0 / 3.0)
    return lowest + jnp.where(speed <= gap_mid, speed, steep)


def travel_kernel(
    times_ref,
    speed_ref,
    refined_ref,
    tab,
    spd,
    swap_in,
    swap_speed,
    halo_in,
    halo_speed,
    edge_out,
    stage,
    arrived,
    start_send,
    start_recv,
    halo_send,
    halo_recv,
    all_send,
    all_recv,
):
    space = lax.axis_index("space")
    sta = lax.axis_index("sta")
    stas = lax.axis_size("sta")
    lines = lax.axis_size("space") // NEAR
    line = space // NEAR
    half = space % NEAR
    depth, rows, lanes = speed_ref.shape
    own = NEAR * depth
    count = own + 2 * HALO
    piece = stage.shape[2]
    member = half * stas + sta
    members = NEAR * stas
    station = NEAR * sta + half
    inside = pl.ds(PAD, rows)
    mesh_id = pl.DeviceIdType.MESH

    def at(other_line, other_half):
        return {"space": ((other_line + lines) % lines) * NEAR + other_half, "sta": sta}

    def member_at(other):
        return {"space": line * NEAR + other // stas, "sta": other % stas}

    barrier = pltpu.get_barrier_semaphore()

    def greet(j, carry):
        pl.semaphore_signal(
            barrier, inc=1, device_id=member_at((member + j) % members), device_id_type=mesh_id
        )
        return carry

    for other_line in (line - 1, line + 1):
        for other_half in range(NEAR):
            pl.semaphore_signal(
                barrier, inc=1, device_id=at(other_line, other_half), device_id_type=mesh_id
            )
    lax.fori_loop(1, members, greet, 0)

    rim = jnp.full((PAD, lanes), BIG, jnp.float32)

    def rims(plane, carry):
        for side in range(2):
            tab[side, plane, pl.ds(0, PAD)] = rim
            tab[side, plane, pl.ds(PAD + rows, PAD)] = rim
        return carry

    lax.fori_loop(0, count, rims, 0)
    pl.semaphore_wait(barrier, members - 1 + 2 * NEAR)

    away = line + 2 * half - 1
    first = half * (depth - HALO)

    def start_copy(j):
        if j == 0:
            src, dst, who = times_ref.at[1 - half], swap_in, at(line, 1 - half)
        elif j == 1:
            src, dst, who = speed_ref, swap_speed, at(line, 1 - half)
        elif j < 4:
            src = times_ref.at[j - 2, pl.ds(first, HALO)]
            dst, who = halo_in.at[0, 1 - half], at(away, j - 2)
        else:
            src = speed_ref.at[pl.ds(first, HALO)]
            dst, who = halo_speed.at[1 - half], at(away, j - 4)
        slot = j if j < 2 else (2 if j < 4 else 4) + (1 - half)
        return pltpu.make_async_remote_copy(
            src_ref=src,
            dst_ref=dst,
            send_sem=start_send.at[j],
            recv_sem=start_recv.at[slot],
            device_id=who,
            device_id_type=mesh_id,
        )

    def start_arrival(slot):
        if slot == 0:
            src, dst = times_ref.at[1 - half], swap_in
        elif slot == 1:
            src, dst = speed_ref, swap_speed
        elif slot < 4:
            src, dst = times_ref.at[0, pl.ds(0, HALO)], halo_in.at[0, slot - 2]
        else:
            src, dst = speed_ref.at[pl.ds(0, HALO)], halo_speed.at[slot - 4]
        return pltpu.make_async_remote_copy(
            src_ref=src,
            dst_ref=dst,
            send_sem=start_send.at[slot],
            recv_sem=start_recv.at[slot],
            device_id=at(line, 1 - half),
            device_id_type=mesh_id,
        )

    for j in (2, 3, 0, 4, 5, 1):
        start_copy(j).start()

    at_lower = line == 0
    at_upper = line == lines - 1

    for i in range(depth):
        tab[0, HALO + half * depth + i, inside] = times_ref[half, i]
        spd[HALO + half * depth + i] = speed_ref[i]
    for slot in range(6):
        start_arrival(slot).wait_recv()
    for i in range(depth):
        tab[0, HALO + (1 - half) * depth + i, inside] = swap_in[i]
        spd[HALO + (1 - half) * depth + i] = swap_speed[i]
    for i in range(HALO):
        spd[i] = halo_speed[0, i]
        spd[HALO + own + i] = halo_speed[1, i]

    def place_halo(exchange, side):
        for i in range(HALO):
            tab[side, i, inside] = jnp.where(at_lower, BIG, halo_in[exchange, 0, i])
            tab[side, HALO + own + i, inside] = jnp.where(at_upper, BIG, halo_in[exchange, 1, i])

    place_halo(0, 0)

    lane = lax.broadcasted_iota(jnp.int32, (rows, lanes), 1)

    def plane_value(side, plane):
        centre = tab[side, plane, inside]
        along_x = jnp.minimum(tab[side, plane - 1, inside], tab[side, plane + 1, inside])
        along_y = jnp.minimum(
            tab[side, plane, pl.ds(PAD - 1, rows)], tab[side, plane, pl.ds(PAD + 1, rows)]
        )
        before = jnp.where(lane == 0, BIG, pltpu.roll(centre, 1, 1))
        after = jnp.where(lane == lanes - 1, BIG, pltpu.roll(centre, lanes - 1, 1))
        along_z = jnp.minimum(before, after)
        value = jnp.minimum(centre, godunov(along_x, along_y, along_z, spd[plane]))
        outside = (at_lower & (plane < HALO)) | (at_upper & (plane >= HALO + own))
        return jnp.maximum(value, jnp.where(outside, BIG, -BIG))

    def sweep(side, total, plane_at, store):
        def one(j, carry):
            plane = plane_at(j)
            store(plane, plane_value(side, plane))
            return carry

        lax.fori_loop(0, total, one, 0)

    def into(side):
        def store(plane, value):
            tab[side, plane, inside] = value

        return store

    def into_stage(plane, value):
        place = plane - HALO
        for j in range(stas):
            stage[(place // depth) * stas + j, place % depth] = value[piece * j : piece * (j + 1)]

    def into_edge(side, exchange, lower):
        def store(plane, value):
            tab[side, plane, inside] = value
            edge_out[exchange, 0 if lower else 1, plane - (HALO if lower else own)] = value

        return store

    def halo_copy(exchange, lower):
        slot = 1 if lower else 0
        return pltpu.make_async_remote_copy(
            src_ref=edge_out.at[exchange - 1, 0 if lower else 1],
            dst_ref=halo_in.at[exchange, slot],
            send_sem=halo_send.at[exchange - 1, slot],
            recv_sem=halo_recv.at[exchange - 1, slot],
            device_id=at(line - 1 if lower else line + 1, half),
            device_id_type=mesh_id,
        )

    def last_round(side, exchange):
        sweep(side, HALO, lambda j: HALO + j, into_edge(1 - side, exchange - 1, True))
        halo_copy(exchange, True).start()
        sweep(side, HALO, lambda j: own + j, into_edge(1 - side, exchange - 1, False))
        halo_copy(exchange, False).start()
        sweep(side, own - 2 * HALO, lambda j: 2 * HALO + j, into(1 - side))

    exchanges = ROUNDS // HALO
    side = 0
    for exchange in range(exchanges):
        final = exchange == exchanges - 1
        if exchange == 0:
            for r in range(HALO - 1):
                sweep(side, count - 2 - 2 * r, lambda j, r=r: r + 1 + j, into(1 - side))
                side = 1 - side
        else:
            start = side
            for r in range(HALO - 1):
                sweep(side, own - 2 - 2 * r, lambda j, r=r: HALO + 1 + r + j, into(1 - side))
                side = 1 - side
            for lower in (True, False):
                halo_copy(exchange, lower).wait()
            side = start
            place_halo(exchange, side)
            for r in range(HALO - 1):
                sweep(
                    side,
                    2 * HALO,
                    lambda j, r=r: jnp.where(j < HALO, r + 1 + j, own - 1 - r + j),
                    into(1 - side),
                )
                side = 1 - side
        if final:
            sweep(side, own, lambda j: HALO + j, into_stage)
        else:
            last_round(side, exchange + 1)
            side = 1 - side

    def block_copy(j):
        other = (member + j) % members
        return pltpu.make_async_remote_copy(
            src_ref=stage.at[other],
            dst_ref=arrived.at[station],
            send_sem=all_send.at[j],
            recv_sem=all_recv.at[station],
            device_id=member_at(other),
            device_id_type=mesh_id,
        )

    def block_arrival(j):
        other = (member + j) % members
        source = NEAR * (other % stas) + other // stas
        return pltpu.make_async_remote_copy(
            src_ref=stage.at[other],
            dst_ref=arrived.at[source],
            send_sem=all_send.at[j],
            recv_sem=all_recv.at[source],
            device_id=member_at(other),
            device_id_type=mesh_id,
        )

    def start_block(j, carry):
        block_copy(j).start()
        return carry

    def end_block(j, carry):
        block_copy(j).wait_send()
        block_arrival(j).wait_recv()
        return carry

    lax.fori_loop(1, members, start_block, 0)
    arrived[station] = stage[member]
    for j in range(6):
        start_copy(j).wait_send()
    lax.fori_loop(1, members, end_block, 0)
    refined_ref[...] = arrived[...]


def refined_tables(coarse_times, speed):
    per_device, depth, rows, lanes = coarse_times.shape
    stas = lax.axis_size("sta")
    stations = per_device * stas
    assert per_device == NEAR and ROUNDS % HALO == 0 and HALO <= depth
    piece = rows // stas
    own = NEAR * depth
    count = own + 2 * HALO
    exchanges = ROUNDS // HALO
    plane = (rows, lanes)
    vmem = pl.BlockSpec(memory_space=pltpu.VMEM)
    dma = pltpu.SemaphoreType.DMA
    return pl.pallas_call(
        travel_kernel,
        out_shape=jax.ShapeDtypeStruct((stations, depth, piece, lanes), jnp.float32),
        in_specs=[vmem, vmem],
        out_specs=vmem,
        scratch_shapes=[
            pltpu.VMEM((2, count, rows + 2 * PAD, lanes), jnp.float32),
            pltpu.VMEM((count,) + plane, jnp.float32),
            pltpu.VMEM((depth,) + plane, jnp.float32),
            pltpu.VMEM((depth,) + plane, jnp.float32),
            pltpu.VMEM((exchanges, 2, HALO) + plane, jnp.float32),
            pltpu.VMEM((2, HALO) + plane, jnp.float32),
            pltpu.VMEM((exchanges - 1, 2, HALO) + plane, jnp.float32),
            pltpu.VMEM((NEAR * stas, depth, piece, lanes), jnp.float32),
            pltpu.VMEM((stations, depth, piece, lanes), jnp.float32),
            dma((6,)),
            dma((6,)),
            dma((exchanges - 1, 2)),
            dma((exchanges - 1, 2)),
            dma((NEAR * stas,)),
            dma((stations,)),
        ],
        compiler_params=pltpu.CompilerParams(collective_id=1, has_side_effects=True),
        name="travel",
    )(coarse_times, speed)


EVENT_TILE = 8


def locate_kernel(
    times_ref,
    picks_ref,
    mask_ref,
    weight_ref,
    peak_ref,
    stats_ref,
    pick_rows,
    mask_rows,
    picked_sum,
    score,
    lane_mass,
    first,
    second,
    local,
    mid,
    send_sem,
    recv_sem,
):
    space = lax.axis_index("space")
    sta = lax.axis_index("sta")
    stas = lax.axis_size("sta")
    lines = lax.axis_size("space") // NEAR
    line = space // NEAR
    member = (space % NEAR) * stas + sta
    members = NEAR * stas

    def member_id(k):
        other = (member + k) % members
        return {"space": line * NEAR + other // stas, "sta": other % stas}

    def line_id(k):
        return {"space": ((line + k) % lines) * NEAR + space % NEAR, "sta": sta}

    barrier = pltpu.get_barrier_semaphore()

    def greet(ids, count):
        def one(k, carry):
            pl.semaphore_signal(barrier, inc=1, device_id=ids(k), device_id_type=pl.DeviceIdType.MESH)
            return carry

        lax.fori_loop(1, count, one, 0)

    greet(member_id, members)
    greet(line_id, lines)

    stations, events = picks_ref.shape
    rows, _, lanes = weight_ref.shape
    blocks = events // lanes

    for b in range(blocks):
        cut = pl.ds(b * lanes, lanes)
        part = picks_ref[:, cut]
        blank = jnp.zeros((lanes - stations, lanes), jnp.float32)
        pick_rows[cut] = jnp.concatenate([part, blank], 0).T
        part = mask_ref[:, cut].astype(jnp.float32)
        blank = jnp.zeros((lanes - 3 * stations, lanes), jnp.float32)
        mask_rows[cut] = jnp.concatenate([part, part, part, blank], 0).T

    chosen = mask_rows[...].astype(jnp.bfloat16)
    blank = jnp.zeros((lanes - 3 * stations, lanes), jnp.float32)

    def pieces(row):
        part = times_ref[pl.ds(row, stations, stride=rows)]
        high = part.astype(jnp.bfloat16).astype(jnp.float32)
        rest = part - high
        middle = rest.astype(jnp.bfloat16).astype(jnp.float32)
        return jnp.concatenate([high, middle, rest - middle, blank], 0).astype(jnp.bfloat16)

    def sums(pair, carry):
        right = jnp.concatenate([pieces(2 * pair), pieces(2 * pair + 1)], 1)
        both = jnp.dot(chosen, right, preferred_element_type=jnp.float32)
        picked_sum[2 * pair] = both[:, :lanes]
        picked_sum[2 * pair + 1] = both[:, lanes:]
        return carry

    lax.fori_loop(0, rows // 2, sums, 0)

    def tile(index, carry):
        cut = pl.ds(pl.multiple_of(index * EVENT_TILE, EVENT_TILE), EVENT_TILE)
        shape = (EVENT_TILE, lanes)
        pick = pick_rows[cut]
        mask = mask_rows[cut]
        arrival = [jnp.broadcast_to(pick[:, s : s + 1], shape) for s in range(stations)]
        seen = [jnp.broadcast_to(mask[:, s : s + 1], shape) for s in range(stations)]
        number = seen[0]
        total = seen[0] * arrival[0]
        for s in range(1, stations):
            number = number + seen[s]
            total = total + seen[s] * arrival[s]

        def row(r, top):
            shift = (total - picked_sum[r, cut]) / number
            misfit = None
            for s in range(stations):
                time = jnp.broadcast_to(times_ref[pl.ds(s * rows + r, 1)], shape)
                deviation = (arrival[s] - time) - shift
                term = seen[s] * (deviation * deviation)
                misfit = term if misfit is None else misfit + term
            value = (-0.5 / (pick_sigma * pick_sigma)) * misfit
            score[r] = value
            return jnp.maximum(top, value)

        top = lax.fori_loop(0, rows, row, jnp.full(shape, -3.0e38, jnp.float32))

        def weigh(r, mass):
            weight = jnp.exp(score[r] - top)
            weight_ref[r, cut] = weight
            return mass + weight

        mass = lax.fori_loop(0, rows, weigh, jnp.zeros(shape, jnp.float32))
        peak_ref[cut] = top
        lane_mass[cut] = mass
        return carry

    lax.fori_loop(0, events // EVENT_TILE, tile, 0)

    for b in range(blocks):
        cut = pl.ds(b * lanes, lanes)
        peak = peak_ref[cut].T
        top = jnp.max(peak, 0, keepdims=True)
        mass = jnp.sum(lane_mass[cut].T * jnp.exp(peak - top), 0, keepdims=True)
        local[pl.ds(b, 1)] = top
        local[pl.ds(blocks + b, 1)] = mass

    pl.semaphore_wait(barrier, members + lines - 2)

    def exchange(src, slots, ids, count, phase):
        def copy(k):
            return pltpu.make_async_remote_copy(
                src_ref=src,
                dst_ref=slots.at[k - 1],
                send_sem=send_sem.at[phase, k - 1],
                recv_sem=recv_sem.at[phase, k - 1],
                device_id=ids(k),
                device_id_type=pl.DeviceIdType.MESH,
            )

        def start(k, carry):
            copy(k).start()
            return carry

        def wait(k, carry):
            copy(k).wait()
            return carry

        lax.fori_loop(1, count, start, 0)
        lax.fori_loop(1, count, wait, 0)

    def merged(top, mass, slots, count):
        best = top
        for k in range(count):
            best = jnp.maximum(best, slots[k, :blocks])
        total = mass * jnp.exp(top - best)
        for k in range(count):
            total = total + slots[k, blocks:] * jnp.exp(slots[k, :blocks] - best)
        return best, total

    exchange(local, first, member_id, members, 0)
    top, mass = merged(local[:blocks], local[blocks:], first, members - 1)
    mid[:blocks] = top
    mid[blocks:] = mass
    exchange(mid, second, line_id, lines, 1)
    top, mass = merged(top, mass, second, lines - 1)
    stats_ref[:blocks] = top
    stats_ref[blocks:] = mass


def density_kernel(weight_ref, peak_ref, stats_ref, out_ref, scale, chunk, sem):
    rows, events, lanes = weight_ref.shape
    blocks = events // lanes
    size = chunk.shape[1] // rows
    for b in range(blocks):
        cut = pl.ds(b * lanes, lanes)
        top = jnp.broadcast_to(stats_ref[pl.ds(b, 1)], (lanes, lanes)).T
        mass = jnp.broadcast_to(stats_ref[pl.ds(blocks + b, 1)], (lanes, lanes)).T
        scale[cut] = jnp.exp(peak_ref[cut] - top) / mass

    def copy(c, slot):
        return pltpu.make_async_copy(
            chunk.at[slot], out_ref.at[pl.ds(c * size * rows, size * rows)], sem.at[slot]
        )

    slots = chunk.shape[0]
    chunks = events // size
    for c in range(chunks):
        slot = c % slots
        if c >= slots:
            copy(c - slots, slot).wait()
        for t in range(size // EVENT_TILE):
            cut = pl.ds(c * size + t * EVENT_TILE, EVENT_TILE)
            factor = scale[cut]
            for r in range(rows):
                chunk[slot, pl.ds(t * EVENT_TILE * rows + r, EVENT_TILE, stride=rows)] = (
                    weight_ref[r, cut] * factor
                )
        copy(c, slot).start()
    for c in range(chunks - slots, chunks):
        copy(c, c % slots).wait()


def event_density(refined, picks, pick_mask):
    stations, depth, piece, lanes = refined.shape
    events = picks.shape[0]
    rows = depth * piece
    assert 3 * stations <= lanes and events % lanes == 0 and rows % 2 == 0
    blocks = events // lanes
    members = NEAR * lax.axis_size("sta")
    lines = lax.axis_size("space") // NEAR
    longest = max(members, lines)
    vmem = pl.BlockSpec(memory_space=pltpu.VMEM)
    wide = (events, lanes)
    message = (2 * blocks, lanes)
    f32 = jnp.float32
    weight, peak, stats = pl.pallas_call(
        locate_kernel,
        out_shape=(
            jax.ShapeDtypeStruct((rows,) + wide, f32),
            jax.ShapeDtypeStruct(wide, f32),
            jax.ShapeDtypeStruct(message, f32),
        ),
        in_specs=[vmem] * 3,
        out_specs=[vmem] * 3,
        scratch_shapes=[
            pltpu.VMEM(wide, f32),
            pltpu.VMEM(wide, f32),
            pltpu.VMEM((rows,) + wide, f32),
            pltpu.VMEM((rows, EVENT_TILE, lanes), f32),
            pltpu.VMEM(wide, f32),
            pltpu.VMEM((members - 1,) + message, f32),
            pltpu.VMEM((lines - 1,) + message, f32),
            pltpu.VMEM(message, f32),
            pltpu.VMEM(message, f32),
            pltpu.SemaphoreType.DMA((2, longest)),
            pltpu.SemaphoreType.DMA((2, longest)),
        ],
        compiler_params=pltpu.CompilerParams(collective_id=0, has_side_effects=True),
        name="locate",
    )(refined.reshape(stations * rows, lanes), picks.T, pick_mask.T)
    density = pl.pallas_call(
        density_kernel,
        out_shape=jax.ShapeDtypeStruct((events * rows, lanes), f32),
        in_specs=[vmem] * 3,
        out_specs=pl.BlockSpec(memory_space=pl.ANY),
        scratch_shapes=[
            pltpu.VMEM(wide, f32),
            pltpu.VMEM((4, 32 * rows, lanes), f32),
            pltpu.SemaphoreType.DMA((4,)),
        ],
        name="density",
    )(weight, peak, stats)
    return density.reshape(events, depth, piece, lanes)


def body(coarse_times, model_map, slowness, picks, pick_mask):
    refined = refined_tables(coarse_times, speed_of(model_map, slowness))
    return refined, event_density(refined, picks, pick_mask)


def solution(mesh):
    placed = (P("sta", "space", None, None), P("space", None, None), P(), P(), P())
    return jax.shard_map(
        body,
        mesh=mesh,
        in_specs=placed,
        out_specs=(P(None, "space", "sta", None), P(None, "space", "sta", None)),
        check_vma=False,
    )
```

```python
import functools

import jax
import jax.numpy as jnp
from jax import lax
from jax.experimental import pallas as pl
from jax.experimental.pallas import tpu as pltpu
from jax.sharding import PartitionSpec as P

ROUNDS = 12

BIG = 1000000.0
pick_sigma = 0.25
grid_step = 1.0
NEAR = 2


HALO = 4
PAD = 8


def godunov(near_one, near_two, near_three, speed):
    small = jnp.minimum(near_one, near_two)
    large = jnp.maximum(near_one, near_two)
    lowest = jnp.minimum(small, near_three)
    highest = jnp.maximum(large, near_three)
    middle = jnp.maximum(small, jnp.minimum(large, near_three))
    gap_mid = middle - lowest
    gap_high = highest - lowest
    spread = highest - middle
    square = speed * speed
    mid_square = gap_mid * gap_mid
    reach = gap_high * gap_high + spread * spread
    two = square <= reach
    inner = jnp.where(two, 2.0 * square, 3.0 * square - reach) - mid_square
    root = jnp.sqrt(jnp.maximum(inner, 0.0))
    base = gap_mid + jnp.where(two, 0.0, gap_high)
    steep = (base + root) * jnp.where(two, 0.5, 1.0 / 3.0)
    return lowest + jnp.where(speed <= gap_mid, speed, steep)


def travel_kernel(
    times_ref,
    map_ref,
    slowness_ref,
    refined_ref,
    speed_ref,
    tab,
    spd,
    swap_in,
    swap_speed,
    halo_in,
    halo_speed,
    edge_out,
    stage,
    arrived,
    start_send,
    start_recv,
    halo_send,
    halo_recv,
    all_send,
    all_recv,
):
    space = lax.axis_index("space")
    sta = lax.axis_index("sta")
    stas = lax.axis_size("sta")
    lines = lax.axis_size("space") // NEAR
    line = space // NEAR
    half = space % NEAR
    depth, rows, lanes = map_ref.shape
    own = NEAR * depth
    count = own + 2 * HALO
    piece = stage.shape[2]
    member = half * stas + sta
    members = NEAR * stas
    station = NEAR * sta + half
    inside = pl.ds(PAD, rows)
    mesh_id = pl.DeviceIdType.MESH

    def at(other_line, other_half):
        return {"space": ((other_line + lines) % lines) * NEAR + other_half, "sta": sta}

    def member_at(other):
        return {"space": line * NEAR + other // stas, "sta": other % stas}

    barrier = pltpu.get_barrier_semaphore()

    def greet(j, carry):
        pl.semaphore_signal(
            barrier, inc=1, device_id=member_at((member + j) % members), device_id_type=mesh_id
        )
        return carry

    for other_line in (line - 1, line + 1):
        for other_half in range(NEAR):
            pl.semaphore_signal(
                barrier, inc=1, device_id=at(other_line, other_half), device_id_type=mesh_id
            )
    lax.fori_loop(1, members, greet, 0)

    rim = jnp.full((PAD, lanes), BIG, jnp.float32)

    def rims(plane, carry):
        for side in range(2):
            tab[side, plane, pl.ds(0, PAD)] = rim
            tab[side, plane, pl.ds(PAD + rows, PAD)] = rim
        return carry

    lax.fori_loop(0, count, rims, 0)

    def look_up(i, carry):
        index = map_ref[i]
        value = jnp.zeros(index.shape, jnp.float32)
        for level in range(slowness_ref.shape[0]):
            value = jnp.where(index == level, slowness_ref[level], value)
        speed_ref[i] = grid_step * value
        return carry

    lax.fori_loop(0, depth, look_up, 0)
    pl.semaphore_wait(barrier, members - 1 + 2 * NEAR)

    away = line + 2 * half - 1
    first = half * (depth - HALO)

    def start_copy(j):
        if j == 0:
            src, dst, who = times_ref.at[1 - half], swap_in, at(line, 1 - half)
        elif j == 1:
            src, dst, who = speed_ref, swap_speed, at(line, 1 - half)
        elif j < 4:
            src = times_ref.at[j - 2, pl.ds(first, HALO)]
            dst, who = halo_in.at[0, 1 - half], at(away, j - 2)
        else:
            src = speed_ref.at[pl.ds(first, HALO)]
            dst, who = halo_speed.at[1 - half], at(away, j - 4)
        slot = j if j < 2 else (2 if j < 4 else 4) + (1 - half)
        return pltpu.make_async_remote_copy(
            src_ref=src,
            dst_ref=dst,
            send_sem=start_send.at[j],
            recv_sem=start_recv.at[slot],
            device_id=who,
            device_id_type=mesh_id,
        )

    def start_arrival(slot):
        if slot == 0:
            src, dst = times_ref.at[1 - half], swap_in
        elif slot == 1:
            src, dst = speed_ref, swap_speed
        elif slot < 4:
            src, dst = times_ref.at[0, pl.ds(0, HALO)], halo_in.at[0, slot - 2]
        else:
            src, dst = speed_ref.at[pl.ds(0, HALO)], halo_speed.at[slot - 4]
        return pltpu.make_async_remote_copy(
            src_ref=src,
            dst_ref=dst,
            send_sem=start_send.at[slot],
            recv_sem=start_recv.at[slot],
            device_id=at(line, 1 - half),
            device_id_type=mesh_id,
        )

    for j in (2, 3, 0, 4, 5, 1):
        start_copy(j).start()

    at_lower = line == 0
    at_upper = line == lines - 1

    for i in range(depth):
        tab[0, HALO + half * depth + i, inside] = times_ref[half, i]
        spd[HALO + half * depth + i] = speed_ref[i]
    for slot in range(6):
        start_arrival(slot).wait_recv()
    for i in range(depth):
        tab[0, HALO + (1 - half) * depth + i, inside] = swap_in[i]
        spd[HALO + (1 - half) * depth + i] = swap_speed[i]
    for i in range(HALO):
        spd[i] = halo_speed[0, i]
        spd[HALO + own + i] = halo_speed[1, i]

    def place_halo(exchange, side):
        for i in range(HALO):
            tab[side, i, inside] = jnp.where(at_lower, BIG, halo_in[exchange, 0, i])
            tab[side, HALO + own + i, inside] = jnp.where(at_upper, BIG, halo_in[exchange, 1, i])

    place_halo(0, 0)

    lane = lax.broadcasted_iota(jnp.int32, (rows, lanes), 1)

    def plane_value(side, plane):
        centre = tab[side, plane, inside]
        along_x = jnp.minimum(tab[side, plane - 1, inside], tab[side, plane + 1, inside])
        along_y = jnp.minimum(
            tab[side, plane, pl.ds(PAD - 1, rows)], tab[side, plane, pl.ds(PAD + 1, rows)]
        )
        before = jnp.where(lane == 0, BIG, pltpu.roll(centre, 1, 1))
        after = jnp.where(lane == lanes - 1, BIG, pltpu.roll(centre, lanes - 1, 1))
        along_z = jnp.minimum(before, after)
        value = jnp.minimum(centre, godunov(along_x, along_y, along_z, spd[plane]))
        outside = (at_lower & (plane < HALO)) | (at_upper & (plane >= HALO + own))
        return jnp.maximum(value, jnp.where(outside, BIG, -BIG))

    def sweep(side, total, plane_at, store):
        def one(j, carry):
            plane = plane_at(j)
            store(plane, plane_value(side, plane))
            return carry

        lax.fori_loop(0, total, one, 0, unroll=2)

    def into(side):
        def store(plane, value):
            tab[side, plane, inside] = value

        return store

    def into_stage(plane, value):
        place = plane - HALO
        for j in range(stas):
            stage[(place // depth) * stas + j, place % depth] = value[piece * j : piece * (j + 1)]

    def into_edge(side, exchange, lower):
        def store(plane, value):
            tab[side, plane, inside] = value
            edge_out[exchange, 0 if lower else 1, plane - (HALO if lower else own)] = value

        return store

    def halo_copy(exchange, lower):
        slot = 1 if lower else 0
        return pltpu.make_async_remote_copy(
            src_ref=edge_out.at[exchange - 1, 0 if lower else 1],
            dst_ref=halo_in.at[exchange, slot],
            send_sem=halo_send.at[exchange - 1, slot],
            recv_sem=halo_recv.at[exchange - 1, slot],
            device_id=at(line - 1 if lower else line + 1, half),
            device_id_type=mesh_id,
        )

    def last_round(side, exchange):
        sweep(side, HALO, lambda j: HALO + j, into_edge(1 - side, exchange - 1, True))
        halo_copy(exchange, True).start()
        sweep(side, HALO, lambda j: own + j, into_edge(1 - side, exchange - 1, False))
        halo_copy(exchange, False).start()
        sweep(side, own - 2 * HALO, lambda j: 2 * HALO + j, into(1 - side))

    exchanges = ROUNDS // HALO
    side = 0
    for exchange in range(exchanges):
        final = exchange == exchanges - 1
        if exchange == 0:
            for r in range(HALO - 1):
                sweep(side, count - 2 - 2 * r, lambda j, r=r: r + 1 + j, into(1 - side))
                side = 1 - side
        else:
            start = side
            for r in range(HALO - 1):
                sweep(side, own - 2 - 2 * r, lambda j, r=r: HALO + 1 + r + j, into(1 - side))
                side = 1 - side
            for lower in (True, False):
                halo_copy(exchange, lower).wait()
            side = start
            place_halo(exchange, side)
            for r in range(HALO - 1):
                sweep(
                    side,
                    2 * HALO,
                    lambda j, r=r: jnp.where(j < HALO, r + 1 + j, own - 1 - r + j),
                    into(1 - side),
                )
                side = 1 - side
        if final:
            sweep(side, own, lambda j: HALO + j, into_stage)
        else:
            last_round(side, exchange + 1)
            side = 1 - side

    def block_copy(j):
        other = (member + j) % members
        return pltpu.make_async_remote_copy(
            src_ref=stage.at[other],
            dst_ref=arrived.at[station],
            send_sem=all_send.at[j],
            recv_sem=all_recv.at[station],
            device_id=member_at(other),
            device_id_type=mesh_id,
        )

    def block_arrival(j):
        other = (member + j) % members
        source = NEAR * (other % stas) + other // stas
        return pltpu.make_async_remote_copy(
            src_ref=stage.at[other],
            dst_ref=arrived.at[source],
            send_sem=all_send.at[j],
            recv_sem=all_recv.at[source],
            device_id=member_at(other),
            device_id_type=mesh_id,
        )

    def start_block(j, carry):
        block_copy(j).start()
        return carry

    def end_block(j, carry):
        block_copy(j).wait_send()
        block_arrival(j).wait_recv()
        return carry

    lax.fori_loop(1, members, start_block, 0)
    arrived[station] = stage[member]
    for j in range(6):
        start_copy(j).wait_send()
    lax.fori_loop(1, members, end_block, 0)
    refined_ref[...] = arrived[...]


def refined_tables(coarse_times, model_map, slowness):
    per_device, depth, rows, lanes = coarse_times.shape
    stas = lax.axis_size("sta")
    stations = per_device * stas
    assert per_device == NEAR and ROUNDS % HALO == 0 and HALO <= depth
    piece = rows // stas
    own = NEAR * depth
    count = own + 2 * HALO
    exchanges = ROUNDS // HALO
    plane = (rows, lanes)
    vmem = pl.BlockSpec(memory_space=pltpu.VMEM)
    dma = pltpu.SemaphoreType.DMA
    return pl.pallas_call(
        travel_kernel,
        out_shape=jax.ShapeDtypeStruct((stations, depth, piece, lanes), jnp.float32),
        in_specs=[vmem, vmem, pl.BlockSpec(memory_space=pltpu.SMEM)],
        out_specs=vmem,
        scratch_shapes=[
            pltpu.VMEM((depth,) + plane, jnp.float32),
            pltpu.VMEM((2, count, rows + 2 * PAD, lanes), jnp.float32),
            pltpu.VMEM((count,) + plane, jnp.float32),
            pltpu.VMEM((depth,) + plane, jnp.float32),
            pltpu.VMEM((depth,) + plane, jnp.float32),
            pltpu.VMEM((exchanges, 2, HALO) + plane, jnp.float32),
            pltpu.VMEM((2, HALO) + plane, jnp.float32),
            pltpu.VMEM((exchanges - 1, 2, HALO) + plane, jnp.float32),
            pltpu.VMEM((NEAR * stas, depth, piece, lanes), jnp.float32),
            pltpu.VMEM((stations, depth, piece, lanes), jnp.float32),
            dma((6,)),
            dma((6,)),
            dma((exchanges - 1, 2)),
            dma((exchanges - 1, 2)),
            dma((NEAR * stas,)),
            dma((stations,)),
        ],
        compiler_params=pltpu.CompilerParams(collective_id=1, has_side_effects=True, vmem_limit_bytes=16 << 20),
        name="travel",
    )(coarse_times, model_map, slowness)


EVENT_TILE = 8
ROW_UNROLL = 5


def locate_kernel(
    times_ref,
    picks_ref,
    mask_ref,
    weight_ref,
    peak_ref,
    stats_ref,
    pick_rows,
    mask_rows,
    picked_sum,
    score,
    lane_mass,
    first,
    second,
    local,
    mid,
    send_sem,
    recv_sem,
):
    space = lax.axis_index("space")
    sta = lax.axis_index("sta")
    stas = lax.axis_size("sta")
    lines = lax.axis_size("space") // NEAR
    line = space // NEAR
    member = (space % NEAR) * stas + sta
    members = NEAR * stas

    def member_id(k):
        other = (member + k) % members
        return {"space": line * NEAR + other // stas, "sta": other % stas}

    def line_id(k):
        return {"space": ((line + k) % lines) * NEAR + space % NEAR, "sta": sta}

    barrier = pltpu.get_barrier_semaphore()

    def greet(ids, count):
        def one(k, carry):
            pl.semaphore_signal(barrier, inc=1, device_id=ids(k), device_id_type=pl.DeviceIdType.MESH)
            return carry

        lax.fori_loop(1, count, one, 0)

    greet(member_id, members)
    greet(line_id, lines)

    stations, events = picks_ref.shape
    rows, _, lanes = weight_ref.shape
    blocks = events // lanes

    for b in range(blocks):
        cut = pl.ds(b * lanes, lanes)
        part = picks_ref[:, cut]
        blank = jnp.zeros((lanes - stations, lanes), jnp.float32)
        pick_rows[cut] = jnp.concatenate([part, blank], 0).T
        part = mask_ref[:, cut].astype(jnp.float32)
        blank = jnp.zeros((lanes - 3 * stations, lanes), jnp.float32)
        mask_rows[cut] = jnp.concatenate([part, part, part, blank], 0).T

    chosen = mask_rows[...].astype(jnp.bfloat16)
    blank = jnp.zeros((lanes - 3 * stations, lanes), jnp.float32)

    def pieces(row):
        part = times_ref[pl.ds(row, stations, stride=rows)]
        high = part.astype(jnp.bfloat16).astype(jnp.float32)
        rest = part - high
        middle = rest.astype(jnp.bfloat16).astype(jnp.float32)
        return jnp.concatenate([high, middle, rest - middle, blank], 0).astype(jnp.bfloat16)

    def sums(pair, carry):
        right = jnp.concatenate([pieces(2 * pair), pieces(2 * pair + 1)], 1)
        both = jnp.dot(chosen, right, preferred_element_type=jnp.float32)
        picked_sum[2 * pair] = both[:, :lanes]
        picked_sum[2 * pair + 1] = both[:, lanes:]
        return carry

    lax.fori_loop(0, rows // 2, sums, 0)

    def tile(index, carry):
        cut = pl.ds(pl.multiple_of(index * EVENT_TILE, EVENT_TILE), EVENT_TILE)
        shape = (EVENT_TILE, lanes)
        pick = pick_rows[cut]
        mask = mask_rows[cut]
        arrival = [jnp.broadcast_to(pick[:, s : s + 1], shape) for s in range(stations)]
        seen = [jnp.broadcast_to(mask[:, s : s + 1], shape) for s in range(stations)]
        number = seen[0]
        total = seen[0] * arrival[0]
        for s in range(1, stations):
            number = number + seen[s]
            total = total + seen[s] * arrival[s]

        share = 1.0 / number
        mean = total * share

        def row(r, top):
            shift = mean - picked_sum[r, cut] * share
            sums = [None] * 4
            for s in range(stations):
                time = jnp.broadcast_to(times_ref[pl.ds(s * rows + r, 1)], shape)
                deviation = (arrival[s] - time) - shift
                term = seen[s] * (deviation * deviation)
                sums[s % 4] = term if sums[s % 4] is None else sums[s % 4] + term
            misfit = functools.reduce(jnp.add, [part for part in sums if part is not None])
            value = (-0.5 / (pick_sigma * pick_sigma)) * misfit
            score[r] = value
            return jnp.maximum(top, value)

        low = jnp.full(shape, -3.0e38, jnp.float32)
        top = lax.fori_loop(0, rows, row, low, unroll=ROW_UNROLL)
        mass = jnp.zeros(shape, jnp.float32)
        for r in range(rows):
            weight = jnp.exp(score[r] - top)
            weight_ref[r, cut] = weight
            mass = mass + weight
        peak_ref[cut] = top
        lane_mass[cut] = mass
        return carry

    lax.fori_loop(0, events // EVENT_TILE, tile, 0)

    for b in range(blocks):
        cut = pl.ds(b * lanes, lanes)
        peak = peak_ref[cut].T
        top = jnp.max(peak, 0, keepdims=True)
        mass = jnp.sum(lane_mass[cut].T * jnp.exp(peak - top), 0, keepdims=True)
        local[pl.ds(b, 1)] = top
        local[pl.ds(blocks + b, 1)] = mass

    pl.semaphore_wait(barrier, members + lines - 2)

    def exchange(src, slots, ids, count, phase):
        def copy(k):
            return pltpu.make_async_remote_copy(
                src_ref=src,
                dst_ref=slots.at[k - 1],
                send_sem=send_sem.at[phase, k - 1],
                recv_sem=recv_sem.at[phase, k - 1],
                device_id=ids(k),
                device_id_type=pl.DeviceIdType.MESH,
            )

        def start(k, carry):
            copy(k).start()
            return carry

        def wait(k, carry):
            copy(k).wait()
            return carry

        lax.fori_loop(1, count, start, 0)
        lax.fori_loop(1, count, wait, 0)

    def merged(top, mass, slots, count):
        best = top
        for k in range(count):
            best = jnp.maximum(best, slots[k, :blocks])
        total = mass * jnp.exp(top - best)
        for k in range(count):
            total = total + slots[k, blocks:] * jnp.exp(slots[k, :blocks] - best)
        return best, total

    exchange(local, first, member_id, members, 0)
    top, mass = merged(local[:blocks], local[blocks:], first, members - 1)
    mid[:blocks] = top
    mid[blocks:] = mass
    exchange(mid, second, line_id, lines, 1)
    top, mass = merged(top, mass, second, lines - 1)
    stats_ref[:blocks] = top
    stats_ref[blocks:] = mass


def density_kernel(weight_ref, peak_ref, stats_ref, out_ref, scale, chunk, sem):
    rows, events, lanes = weight_ref.shape
    blocks = events // lanes
    size = chunk.shape[1] // rows
    for b in range(blocks):
        cut = pl.ds(b * lanes, lanes)
        top = jnp.broadcast_to(stats_ref[pl.ds(b, 1)], (lanes, lanes)).T
        mass = jnp.broadcast_to(stats_ref[pl.ds(blocks + b, 1)], (lanes, lanes)).T
        scale[cut] = jnp.exp(peak_ref[cut] - top) / mass

    def copy(c, slot):
        return pltpu.make_async_copy(
            chunk.at[slot], out_ref.at[pl.ds(c * size * rows, size * rows)], sem.at[slot]
        )

    slots = chunk.shape[0]
    chunks = events // size
    for c in range(chunks):
        slot = c % slots
        if c >= slots:
            copy(c - slots, slot).wait()
        for t in range(size // EVENT_TILE):
            cut = pl.ds(c * size + t * EVENT_TILE, EVENT_TILE)
            factor = scale[cut]
            for r in range(rows):
                chunk[slot, pl.ds(t * EVENT_TILE * rows + r, EVENT_TILE, stride=rows)] = (
                    weight_ref[r, cut] * factor
                )
        copy(c, slot).start()
    for c in range(chunks - slots, chunks):
        copy(c, c % slots).wait()


def event_density(refined, picks, pick_mask):
    stations, depth, piece, lanes = refined.shape
    events = picks.shape[0]
    rows = depth * piece
    assert 3 * stations <= lanes and events % lanes == 0 and rows % 2 == 0
    blocks = events // lanes
    members = NEAR * lax.axis_size("sta")
    lines = lax.axis_size("space") // NEAR
    longest = max(members, lines)
    vmem = pl.BlockSpec(memory_space=pltpu.VMEM)
    wide = (events, lanes)
    message = (2 * blocks, lanes)
    f32 = jnp.float32
    weight, peak, stats = pl.pallas_call(
        locate_kernel,
        out_shape=(
            jax.ShapeDtypeStruct((rows,) + wide, f32),
            jax.ShapeDtypeStruct(wide, f32),
            jax.ShapeDtypeStruct(message, f32),
        ),
        in_specs=[vmem] * 3,
        out_specs=[vmem] * 3,
        scratch_shapes=[
            pltpu.VMEM(wide, f32),
            pltpu.VMEM(wide, f32),
            pltpu.VMEM((rows,) + wide, f32),
            pltpu.VMEM((rows, EVENT_TILE, lanes), f32),
            pltpu.VMEM(wide, f32),
            pltpu.VMEM((members - 1,) + message, f32),
            pltpu.VMEM((lines - 1,) + message, f32),
            pltpu.VMEM(message, f32),
            pltpu.VMEM(message, f32),
            pltpu.SemaphoreType.DMA((2, longest)),
            pltpu.SemaphoreType.DMA((2, longest)),
        ],
        compiler_params=pltpu.CompilerParams(collective_id=0, has_side_effects=True, vmem_limit_bytes=16 << 20),
        name="locate",
    )(refined.reshape(stations * rows, lanes), picks.T, pick_mask.T)
    density = pl.pallas_call(
        density_kernel,
        out_shape=jax.ShapeDtypeStruct((events * rows, lanes), f32),
        in_specs=[vmem] * 3,
        out_specs=pl.BlockSpec(memory_space=pl.ANY),
        scratch_shapes=[
            pltpu.VMEM(wide, f32),
            pltpu.VMEM((4, 32 * rows, lanes), f32),
            pltpu.SemaphoreType.DMA((4,)),
        ],
        compiler_params=pltpu.CompilerParams(vmem_limit_bytes=16 << 20),
        name="density",
    )(weight, peak, stats)
    return density.reshape(events, depth, piece, lanes)


def body(coarse_times, model_map, slowness, picks, pick_mask):
    refined = refined_tables(coarse_times, model_map, slowness)
    return refined, event_density(refined, picks, pick_mask)


def solution(mesh):
    placed = (P("sta", "space", None, None), P("space", None, None), P(), P(), P())
    return jax.shard_map(
        body,
        mesh=mesh,
        in_specs=placed,
        out_specs=(P(None, "space", "sta", None), P(None, "space", "sta", None)),
        check_vma=False,
    )
```

```python
import functools

import jax
import jax.numpy as jnp
from jax import lax
from jax.experimental import pallas as pl
from jax.experimental.pallas import tpu as pltpu
from jax.sharding import PartitionSpec as P

ROUNDS = 12

BIG = 1000000.0
pick_sigma = 0.25
grid_step = 1.0
NEAR = 2


HALO = 4
PAD = 8


def godunov(near_one, near_two, near_three, speed):
    small = jnp.minimum(near_one, near_two)
    large = jnp.maximum(near_one, near_two)
    lowest = jnp.minimum(small, near_three)
    highest = jnp.maximum(large, near_three)
    middle = jnp.maximum(small, jnp.minimum(large, near_three))
    gap_mid = middle - lowest
    gap_high = highest - lowest
    spread = highest - middle
    square = speed * speed
    mid_square = gap_mid * gap_mid
    reach = gap_high * gap_high + spread * spread
    two = square <= reach
    inner = jnp.where(two, 2.0 * square, 3.0 * square - reach) - mid_square
    root = jnp.sqrt(jnp.maximum(inner, 0.0))
    base = gap_mid + jnp.where(two, 0.0, gap_high)
    steep = (base + root) * jnp.where(two, 0.5, 1.0 / 3.0)
    return lowest + jnp.where(speed <= gap_mid, speed, steep)


def event_rows(picks_ref, mask_ref, pick_rows, mask_rows):
    stations, events = picks_ref.shape
    lanes = pick_rows.shape[1]
    for b in range(events // lanes):
        cut = pl.ds(b * lanes, lanes)
        part = picks_ref[:, cut]
        blank = jnp.zeros((lanes - stations, lanes), jnp.float32)
        pick_rows[cut] = jnp.concatenate([part, blank], 0).T
        part = mask_ref[:, cut].astype(jnp.float32)
        blank = jnp.zeros((lanes - 3 * stations, lanes), jnp.float32)
        mask_rows[cut] = jnp.concatenate([part, part, part, blank], 0).T


def travel_kernel(
    times_ref,
    map_hbm,
    slowness_hbm,
    picks_hbm,
    mask_hbm,
    refined_ref,
    pick_rows,
    mask_rows,
    own_times,
    map_ref,
    slowness_ref,
    picks_ref,
    mask_ref,
    load_sem,
    speed_ref,
    tab,
    spd,
    swap_in,
    swap_speed,
    halo_in,
    halo_speed,
    edge_out,
    stage,
    arrived,
    start_send,
    start_recv,
    halo_send,
    halo_recv,
    all_send,
    all_recv,
):
    space = lax.axis_index("space")
    sta = lax.axis_index("sta")
    stas = lax.axis_size("sta")
    lines = lax.axis_size("space") // NEAR
    line = space // NEAR
    half = space % NEAR
    depth, rows, lanes = map_ref.shape
    own = NEAR * depth
    count = own + 2 * HALO
    piece = stage.shape[2]
    member = half * stas + sta
    members = NEAR * stas
    station = NEAR * sta + half
    inside = pl.ds(PAD, rows)
    mesh_id = pl.DeviceIdType.MESH

    loads = [
        pltpu.make_async_copy(src, dst, load_sem.at[i])
        for i, (src, dst) in enumerate(
            (
                (map_hbm, map_ref),
                (slowness_hbm, slowness_ref),
                (times_ref.at[half], own_times),
                (picks_hbm, picks_ref),
                (mask_hbm, mask_ref),
            )
        )
    ]
    for load in loads:
        load.start()

    def at(other_line, other_half):
        return {"space": ((other_line + lines) % lines) * NEAR + other_half, "sta": sta}

    def member_at(other):
        return {"space": line * NEAR + other // stas, "sta": other % stas}

    barrier = pltpu.get_barrier_semaphore()

    def greet(j, carry):
        pl.semaphore_signal(
            barrier, inc=1, device_id=member_at((member + j) % members), device_id_type=mesh_id
        )
        return carry

    for other_line in (line - 1, line + 1):
        for other_half in range(NEAR):
            pl.semaphore_signal(
                barrier, inc=1, device_id=at(other_line, other_half), device_id_type=mesh_id
            )
    lax.fori_loop(1, members, greet, 0)

    rim = jnp.full((PAD, lanes), BIG, jnp.float32)

    def rims(plane, carry):
        for side in range(2):
            tab[side, plane, pl.ds(0, PAD)] = rim
            tab[side, plane, pl.ds(PAD + rows, PAD)] = rim
        return carry

    lax.fori_loop(0, count, rims, 0)

    def look_up(i, carry):
        index = map_ref[i]
        value = jnp.zeros(index.shape, jnp.float32)
        for level in range(slowness_ref.shape[0]):
            value = jnp.where(index == level, slowness_ref[level], value)
        speed_ref[i] = grid_step * value
        return carry

    loads[0].wait()
    loads[1].wait()
    lax.fori_loop(0, depth, look_up, 0)
    pl.semaphore_wait(barrier, members - 1 + 2 * NEAR)

    away = line + 2 * half - 1
    first = half * (depth - HALO)

    def start_copy(j):
        if j == 0:
            src, dst, who = times_ref.at[1 - half], swap_in, at(line, 1 - half)
        elif j == 1:
            src, dst, who = speed_ref, swap_speed, at(line, 1 - half)
        elif j < 4:
            src = times_ref.at[j - 2, pl.ds(first, HALO)]
            dst, who = halo_in.at[0, 1 - half], at(away, j - 2)
        else:
            src = speed_ref.at[pl.ds(first, HALO)]
            dst, who = halo_speed.at[1 - half], at(away, j - 4)
        slot = j if j < 2 else (2 if j < 4 else 4) + (1 - half)
        return pltpu.make_async_remote_copy(
            src_ref=src,
            dst_ref=dst,
            send_sem=start_send.at[j],
            recv_sem=start_recv.at[slot],
            device_id=who,
            device_id_type=mesh_id,
        )

    def start_arrival(slot):
        if slot == 0:
            src, dst = times_ref.at[1 - half], swap_in
        elif slot == 1:
            src, dst = speed_ref, swap_speed
        elif slot < 4:
            src, dst = times_ref.at[0, pl.ds(0, HALO)], halo_in.at[0, slot - 2]
        else:
            src, dst = speed_ref.at[pl.ds(0, HALO)], halo_speed.at[slot - 4]
        return pltpu.make_async_remote_copy(
            src_ref=src,
            dst_ref=dst,
            send_sem=start_send.at[slot],
            recv_sem=start_recv.at[slot],
            device_id=at(line, 1 - half),
            device_id_type=mesh_id,
        )

    for j in (0, 2, 3, 1, 4, 5):
        start_copy(j).start()

    at_lower = line == 0
    at_upper = line == lines - 1

    loads[3].wait()
    loads[4].wait()
    event_rows(picks_ref, mask_ref, pick_rows, mask_rows)
    loads[2].wait()
    for i in range(depth):
        tab[0, HALO + half * depth + i, inside] = own_times[i]
        spd[HALO + half * depth + i] = speed_ref[i]
    for slot in range(2):
        start_arrival(slot).wait_recv()
    for i in range(depth):
        tab[0, HALO + (1 - half) * depth + i, inside] = swap_in[i]
        spd[HALO + (1 - half) * depth + i] = swap_speed[i]

    def place_halo(exchange, side):
        for i in range(HALO):
            tab[side, i, inside] = jnp.where(at_lower, BIG, halo_in[exchange, 0, i])
            tab[side, HALO + own + i, inside] = jnp.where(at_upper, BIG, halo_in[exchange, 1, i])

    lane = lax.broadcasted_iota(jnp.int32, (rows, lanes), 1)

    def plane_value(side, plane):
        centre = tab[side, plane, inside]
        along_x = jnp.minimum(tab[side, plane - 1, inside], tab[side, plane + 1, inside])
        along_y = jnp.minimum(
            tab[side, plane, pl.ds(PAD - 1, rows)], tab[side, plane, pl.ds(PAD + 1, rows)]
        )
        before = jnp.where(lane == 0, BIG, pltpu.roll(centre, 1, 1))
        after = jnp.where(lane == lanes - 1, BIG, pltpu.roll(centre, lanes - 1, 1))
        along_z = jnp.minimum(before, after)
        value = jnp.minimum(centre, godunov(along_x, along_y, along_z, spd[plane]))
        outside = (at_lower & (plane < HALO)) | (at_upper & (plane >= HALO + own))
        return jnp.maximum(value, jnp.where(outside, BIG, -BIG))

    def sweep(side, total, plane_at, store):
        def one(j, carry):
            plane = plane_at(j)
            store(plane, plane_value(side, plane))
            return carry

        lax.fori_loop(0, total, one, 0, unroll=2)

    def into(side):
        def store(plane, value):
            tab[side, plane, inside] = value

        return store

    def into_stage(plane, value):
        place = plane - HALO
        for j in range(stas):
            stage[(place // depth) * stas + j, place % depth] = value[piece * j : piece * (j + 1)]

    def into_edge(side, exchange, lower):
        def store(plane, value):
            tab[side, plane, inside] = value
            edge_out[exchange, 0 if lower else 1, plane - (HALO if lower else own)] = value

        return store

    def halo_copy(exchange, lower):
        slot = 1 if lower else 0
        return pltpu.make_async_remote_copy(
            src_ref=edge_out.at[exchange - 1, 0 if lower else 1],
            dst_ref=halo_in.at[exchange, slot],
            send_sem=halo_send.at[exchange - 1, slot],
            recv_sem=halo_recv.at[exchange - 1, slot],
            device_id=at(line - 1 if lower else line + 1, half),
            device_id_type=mesh_id,
        )

    def last_round(side, exchange):
        sweep(side, HALO, lambda j: HALO + j, into_edge(1 - side, exchange - 1, True))
        halo_copy(exchange, True).start()
        sweep(side, HALO, lambda j: own + j, into_edge(1 - side, exchange - 1, False))
        halo_copy(exchange, False).start()
        sweep(side, own - 2 * HALO, lambda j: 2 * HALO + j, into(1 - side))

    exchanges = ROUNDS // HALO
    side = 0
    for exchange in range(exchanges):
        final = exchange == exchanges - 1
        start = side
        for r in range(HALO - 1):
            sweep(side, own - 2 - 2 * r, lambda j, r=r: HALO + 1 + r + j, into(1 - side))
            side = 1 - side
        if exchange == 0:
            for slot in range(2, 6):
                start_arrival(slot).wait_recv()
            for i in range(HALO):
                spd[i] = halo_speed[0, i]
                spd[HALO + own + i] = halo_speed[1, i]
        else:
            for lower in (True, False):
                halo_copy(exchange, lower).wait()
        side = start
        place_halo(exchange, side)
        for r in range(HALO - 1):
            sweep(
                side,
                2 * HALO,
                lambda j, r=r: jnp.where(j < HALO, r + 1 + j, own - 1 - r + j),
                into(1 - side),
            )
            side = 1 - side
        if final:
            sweep(side, own, lambda j: HALO + j, into_stage)
        else:
            last_round(side, exchange + 1)
            side = 1 - side

    def block_copy(j):
        other = (member + j) % members
        return pltpu.make_async_remote_copy(
            src_ref=stage.at[other],
            dst_ref=arrived.at[station],
            send_sem=all_send.at[j],
            recv_sem=all_recv.at[station],
            device_id=member_at(other),
            device_id_type=mesh_id,
        )

    def block_arrival(j):
        other = (member + j) % members
        source = NEAR * (other % stas) + other // stas
        return pltpu.make_async_remote_copy(
            src_ref=stage.at[other],
            dst_ref=arrived.at[source],
            send_sem=all_send.at[j],
            recv_sem=all_recv.at[source],
            device_id=member_at(other),
            device_id_type=mesh_id,
        )

    def start_block(j, carry):
        block_copy(j).start()
        return carry

    def end_block(j, carry):
        block_copy(j).wait_send()
        block_arrival(j).wait_recv()
        return carry

    lax.fori_loop(1, members, start_block, 0)
    arrived[station] = stage[member]
    for j in range(6):
        start_copy(j).wait_send()
    lax.fori_loop(1, members, end_block, 0)
    refined_ref[...] = arrived[...]


def refined_tables(coarse_times, model_map, slowness, picks, pick_mask):
    per_device, depth, rows, lanes = coarse_times.shape
    stas = lax.axis_size("sta")
    stations = per_device * stas
    assert per_device == NEAR and ROUNDS % HALO == 0 and HALO <= depth
    piece = rows // stas
    own = NEAR * depth
    count = own + 2 * HALO
    exchanges = ROUNDS // HALO
    plane = (rows, lanes)
    vmem = pl.BlockSpec(memory_space=pltpu.VMEM)
    dma = pltpu.SemaphoreType.DMA
    events = picks.shape[0]
    wide = (events, lanes)
    hbm = pl.BlockSpec(memory_space=pltpu.HBM)
    return pl.pallas_call(
        travel_kernel,
        out_shape=(
            jax.ShapeDtypeStruct((stations, depth, piece, lanes), jnp.float32),
            jax.ShapeDtypeStruct(wide, jnp.float32),
            jax.ShapeDtypeStruct(wide, jnp.float32),
        ),
        in_specs=[hbm] * 5,
        out_specs=[vmem] * 3,
        scratch_shapes=[
            pltpu.VMEM((depth,) + plane, jnp.float32),
            pltpu.VMEM((depth,) + plane, jnp.int32),
            pltpu.SMEM(slowness.shape, jnp.float32),
            pltpu.VMEM((stations, events), jnp.float32),
            pltpu.VMEM((stations, events), jnp.int32),
            dma((5,)),
            pltpu.VMEM((depth,) + plane, jnp.float32),
            pltpu.VMEM((2, count, rows + 2 * PAD, lanes), jnp.float32),
            pltpu.VMEM((count,) + plane, jnp.float32),
            pltpu.VMEM((depth,) + plane, jnp.float32),
            pltpu.VMEM((depth,) + plane, jnp.float32),
            pltpu.VMEM((exchanges, 2, HALO) + plane, jnp.float32),
            pltpu.VMEM((2, HALO) + plane, jnp.float32),
            pltpu.VMEM((exchanges - 1, 2, HALO) + plane, jnp.float32),
            pltpu.VMEM((NEAR * stas, depth, piece, lanes), jnp.float32),
            pltpu.VMEM((stations, depth, piece, lanes), jnp.float32),
            dma((6,)),
            dma((6,)),
            dma((exchanges - 1, 2)),
            dma((exchanges - 1, 2)),
            dma((NEAR * stas,)),
            dma((stations,)),
        ],
        compiler_params=pltpu.CompilerParams(collective_id=1, has_side_effects=True, vmem_limit_bytes=16 << 20),
        name="travel",
    )(*[pltpu.with_memory_space_constraint(x, pltpu.HBM) for x in (coarse_times, model_map, slowness, picks.T, pick_mask.T)])


EVENT_TILE = 8
ROW_UNROLL = 5


def locate_kernel(
    times_ref,
    pick_rows,
    mask_rows,
    weight_ref,
    peak_ref,
    stats_ref,
    picked_sum,
    score,
    lane_mass,
    first,
    second,
    local,
    mid,
    send_sem,
    recv_sem,
):
    space = lax.axis_index("space")
    sta = lax.axis_index("sta")
    stas = lax.axis_size("sta")
    lines = lax.axis_size("space") // NEAR
    line = space // NEAR
    member = (space % NEAR) * stas + sta
    members = NEAR * stas

    def member_id(k):
        other = (member + k) % members
        return {"space": line * NEAR + other // stas, "sta": other % stas}

    def line_id(k):
        return {"space": ((line + k) % lines) * NEAR + space % NEAR, "sta": sta}

    barrier = pltpu.get_barrier_semaphore()

    def greet(ids, count):
        def one(k, carry):
            pl.semaphore_signal(barrier, inc=1, device_id=ids(k), device_id_type=pl.DeviceIdType.MESH)
            return carry

        lax.fori_loop(1, count, one, 0)

    greet(member_id, members)
    greet(line_id, lines)

    rows, events, lanes = weight_ref.shape
    stations = times_ref.shape[0] // rows
    blocks = events // lanes

    chosen = mask_rows[...].astype(jnp.bfloat16)
    blank = jnp.zeros((lanes - 3 * stations, lanes), jnp.float32)

    def pieces(row):
        part = times_ref[pl.ds(row, stations, stride=rows)]
        high = part.astype(jnp.bfloat16).astype(jnp.float32)
        rest = part - high
        middle = rest.astype(jnp.bfloat16).astype(jnp.float32)
        return jnp.concatenate([high, middle, rest - middle, blank], 0).astype(jnp.bfloat16)

    def sums(pair, carry):
        right = jnp.concatenate([pieces(2 * pair), pieces(2 * pair + 1)], 1)
        both = jnp.dot(chosen, right, preferred_element_type=jnp.float32)
        picked_sum[2 * pair] = both[:, :lanes]
        picked_sum[2 * pair + 1] = both[:, lanes:]
        return carry

    lax.fori_loop(0, rows // 2, sums, 0)

    def tile(index, carry):
        cut = pl.ds(pl.multiple_of(index * EVENT_TILE, EVENT_TILE), EVENT_TILE)
        shape = (EVENT_TILE, lanes)
        pick = pick_rows[cut]
        mask = mask_rows[cut]
        arrival = [jnp.broadcast_to(pick[:, s : s + 1], shape) for s in range(stations)]
        seen = [jnp.broadcast_to(mask[:, s : s + 1], shape) for s in range(stations)]
        number = seen[0]
        total = seen[0] * arrival[0]
        for s in range(1, stations):
            number = number + seen[s]
            total = total + seen[s] * arrival[s]

        share = 1.0 / number
        mean = total * share

        def row(r, top):
            shift = mean - picked_sum[r, cut] * share
            sums = [None] * 4
            for s in range(stations):
                time = jnp.broadcast_to(times_ref[pl.ds(s * rows + r, 1)], shape)
                deviation = (arrival[s] - time) - shift
                term = seen[s] * (deviation * deviation)
                sums[s % 4] = term if sums[s % 4] is None else sums[s % 4] + term
            misfit = functools.reduce(jnp.add, [part for part in sums if part is not None])
            value = (-0.5 / (pick_sigma * pick_sigma)) * misfit
            score[r] = value
            return jnp.maximum(top, value)

        low = jnp.full(shape, -3.0e38, jnp.float32)
        top = lax.fori_loop(0, rows, row, low, unroll=ROW_UNROLL)
        mass = jnp.zeros(shape, jnp.float32)
        for r in range(rows):
            weight = jnp.exp(score[r] - top)
            weight_ref[r, cut] = weight
            mass = mass + weight
        peak_ref[cut] = top
        lane_mass[cut] = mass
        return carry

    lax.fori_loop(0, events // EVENT_TILE, tile, 0)

    for b in range(blocks):
        cut = pl.ds(b * lanes, lanes)
        peak = peak_ref[cut].T
        top = jnp.max(peak, 0, keepdims=True)
        mass = jnp.sum(lane_mass[cut].T * jnp.exp(peak - top), 0, keepdims=True)
        local[pl.ds(b, 1)] = top
        local[pl.ds(blocks + b, 1)] = mass

    pl.semaphore_wait(barrier, members + lines - 2)

    def exchange(src, slots, ids, count, phase):
        def copy(k):
            return pltpu.make_async_remote_copy(
                src_ref=src,
                dst_ref=slots.at[k - 1],
                send_sem=send_sem.at[phase, k - 1],
                recv_sem=recv_sem.at[phase, k - 1],
                device_id=ids(k),
                device_id_type=pl.DeviceIdType.MESH,
            )

        def start(k, carry):
            copy(k).start()
            return carry

        def wait(k, carry):
            copy(k).wait()
            return carry

        lax.fori_loop(1, count, start, 0)
        lax.fori_loop(1, count, wait, 0)

    def merged(top, mass, slots, count):
        best = top
        for k in range(count):
            best = jnp.maximum(best, slots[k, :blocks])
        total = mass * jnp.exp(top - best)
        for k in range(count):
            total = total + slots[k, blocks:] * jnp.exp(slots[k, :blocks] - best)
        return best, total

    exchange(local, first, member_id, members, 0)
    top, mass = merged(local[:blocks], local[blocks:], first, members - 1)
    mid[:blocks] = top
    mid[blocks:] = mass
    exchange(mid, second, line_id, lines, 1)
    top, mass = merged(top, mass, second, lines - 1)
    stats_ref[:blocks] = top
    stats_ref[blocks:] = mass


def density_kernel(
    weight_ref, peak_ref, stats_ref, refined_ref, out_ref, table_ref, scale, chunk, sem, table_sem
):
    table = pltpu.make_async_copy(refined_ref, table_ref, table_sem)
    table.start()
    rows, events, lanes = weight_ref.shape
    blocks = events // lanes
    size = chunk.shape[1] // rows
    for b in range(blocks):
        cut = pl.ds(b * lanes, lanes)
        top = jnp.broadcast_to(stats_ref[pl.ds(b, 1)], (lanes, lanes)).T
        mass = jnp.broadcast_to(stats_ref[pl.ds(blocks + b, 1)], (lanes, lanes)).T
        scale[cut] = jnp.exp(peak_ref[cut] - top) / mass

    def copy(c, slot):
        return pltpu.make_async_copy(
            chunk.at[slot], out_ref.at[pl.ds(c * size * rows, size * rows)], sem.at[slot]
        )

    slots = chunk.shape[0]
    chunks = events // size
    for c in range(chunks):
        slot = c % slots
        if c >= slots:
            copy(c - slots, slot).wait()
        for t in range(size // EVENT_TILE):
            cut = pl.ds(c * size + t * EVENT_TILE, EVENT_TILE)
            factor = scale[cut]
            for r in range(rows):
                chunk[slot, pl.ds(t * EVENT_TILE * rows + r, EVENT_TILE, stride=rows)] = (
                    weight_ref[r, cut] * factor
                )
        copy(c, slot).start()
    for c in range(chunks - slots, chunks):
        copy(c, c % slots).wait()
    table.wait()


def event_density(refined, pick_rows, mask_rows):
    stations, depth, piece, lanes = refined.shape
    events = pick_rows.shape[0]
    rows = depth * piece
    assert 3 * stations <= lanes and events % lanes == 0 and rows % 2 == 0
    blocks = events // lanes
    members = NEAR * lax.axis_size("sta")
    lines = lax.axis_size("space") // NEAR
    longest = max(members, lines)
    vmem = pl.BlockSpec(memory_space=pltpu.VMEM)
    wide = (events, lanes)
    message = (2 * blocks, lanes)
    f32 = jnp.float32
    weight, peak, stats = pl.pallas_call(
        locate_kernel,
        out_shape=(
            jax.ShapeDtypeStruct((rows,) + wide, f32),
            jax.ShapeDtypeStruct(wide, f32),
            jax.ShapeDtypeStruct(message, f32),
        ),
        in_specs=[vmem] * 3,
        out_specs=[vmem] * 3,
        scratch_shapes=[
            pltpu.VMEM((rows,) + wide, f32),
            pltpu.VMEM((rows, EVENT_TILE, lanes), f32),
            pltpu.VMEM(wide, f32),
            pltpu.VMEM((members - 1,) + message, f32),
            pltpu.VMEM((lines - 1,) + message, f32),
            pltpu.VMEM(message, f32),
            pltpu.VMEM(message, f32),
            pltpu.SemaphoreType.DMA((2, longest)),
            pltpu.SemaphoreType.DMA((2, longest)),
        ],
        compiler_params=pltpu.CompilerParams(collective_id=0, has_side_effects=True, vmem_limit_bytes=16 << 20),
        name="locate",
    )(refined.reshape(stations * rows, lanes), pick_rows, mask_rows)
    density, table = pl.pallas_call(
        density_kernel,
        out_shape=(
            jax.ShapeDtypeStruct((events * rows, lanes), f32),
            jax.ShapeDtypeStruct(refined.shape, f32),
        ),
        in_specs=[vmem] * 4,
        out_specs=[pl.BlockSpec(memory_space=pltpu.HBM)] * 2,
        scratch_shapes=[
            pltpu.VMEM(wide, f32),
            pltpu.VMEM((4, 32 * rows, lanes), f32),
            pltpu.SemaphoreType.DMA((4,)),
            pltpu.SemaphoreType.DMA,
        ],
        compiler_params=pltpu.CompilerParams(vmem_limit_bytes=16 << 20),
        name="density",
    )(weight, peak, stats, refined)
    return table, density.reshape(events, depth, piece, lanes)


def body(coarse_times, model_map, slowness, picks, pick_mask):
    refined, pick_rows, mask_rows = refined_tables(
        coarse_times, model_map, slowness, picks, pick_mask
    )
    return event_density(refined, pick_rows, mask_rows)


def solution(mesh):
    placed = (P("sta", "space", None, None), P("space", None, None), P(), P(), P())
    return jax.shard_map(
        body,
        mesh=mesh,
        in_specs=placed,
        out_specs=(P(None, "space", "sta", None), P(None, "space", "sta", None)),
        check_vma=False,
    )
```

```python
import functools

import jax
import jax.numpy as jnp
from jax import lax
from jax.experimental import pallas as pl
from jax.experimental.pallas import tpu as pltpu
from jax.sharding import PartitionSpec as P

ROUNDS = 12

BIG = 1000000.0
pick_sigma = 0.25
grid_step = 1.0
NEAR = 2


HALO = 4
PAD = 8
EVENT_TILE = 8
ROW_UNROLL = 5


def godunov(near_one, near_two, near_three, speed):
    small = jnp.minimum(near_one, near_two)
    large = jnp.maximum(near_one, near_two)
    lowest = jnp.minimum(small, near_three)
    highest = jnp.maximum(large, near_three)
    middle = jnp.maximum(small, jnp.minimum(large, near_three))
    gap_mid = middle - lowest
    gap_high = highest - lowest
    spread = highest - middle
    square = speed * speed
    excess = square - (gap_high * gap_high + spread * spread)
    two = excess <= 0.0
    inner = (square + square - gap_mid * gap_mid) + jnp.maximum(excess, 0.0)
    inner = jnp.maximum(inner, 1e-30)
    base = gap_mid + inner * lax.rsqrt(inner)
    steep = jnp.where(two, 0.5 * base, (base + gap_high) * (1.0 / 3.0))
    return lowest + jnp.where(speed <= gap_mid, speed, steep)


def event_rows(picks_ref, mask_ref, pick_rows, mask_rows):
    stations, events = picks_ref.shape
    lanes = pick_rows.shape[1]
    for b in range(events // lanes):
        cut = pl.ds(b * lanes, lanes)
        part = picks_ref[:, cut]
        blank = jnp.zeros((lanes - stations, lanes), jnp.float32)
        pick_rows[cut] = jnp.concatenate([part, blank], 0).T
        part = mask_ref[:, cut].astype(jnp.float32)
        blank = jnp.zeros((lanes - 3 * stations, lanes), jnp.float32)
        mask_rows[cut] = jnp.concatenate([part, part, part, blank], 0).T


def spread_events(stations, pick_rows, mask_rows, arrival_ref, seen_ref, mean_ref, share_ref):
    events, lanes = pick_rows.shape
    shape = (EVENT_TILE, lanes)

    def tile(index, carry):
        cut = pl.ds(pl.multiple_of(index * EVENT_TILE, EVENT_TILE), EVENT_TILE)
        pick = pick_rows[cut]
        mask = mask_rows[cut]
        number = None
        for s in range(stations):
            arrival = jnp.broadcast_to(pick[:, s : s + 1], shape)
            seen = jnp.broadcast_to(mask[:, s : s + 1], shape)
            arrival_ref[s, cut] = arrival
            seen_ref[s, cut] = seen
            number = seen if number is None else number + seen
            total = seen * arrival if s == 0 else total + seen * arrival
        share = 1.0 / number
        mean_ref[cut] = total * share
        share_ref[cut] = share
        return carry

    lax.fori_loop(0, events // EVENT_TILE, tile, 0)


def travel_kernel(
    times_ref,
    map_hbm,
    slowness_hbm,
    picks_hbm,
    mask_hbm,
    refined_ref,
    mask_rows,
    arrival_ref,
    seen_ref,
    mean_ref,
    share_ref,
    pick_rows,
    own_times,
    map_ref,
    slowness_ref,
    picks_ref,
    mask_ref,
    load_sem,
    speed_ref,
    tab,
    spd,
    swap_in,
    swap_speed,
    halo_in,
    halo_speed,
    edge_out,
    stage,
    arrived,
    start_send,
    start_recv,
    halo_send,
    halo_recv,
    all_send,
    all_recv,
):
    space = lax.axis_index("space")
    sta = lax.axis_index("sta")
    stas = lax.axis_size("sta")
    lines = lax.axis_size("space") // NEAR
    line = space // NEAR
    half = space % NEAR
    depth, rows, lanes = map_ref.shape
    own = NEAR * depth
    count = own + 2 * HALO
    piece = stage.shape[2]
    member = half * stas + sta
    members = NEAR * stas
    station = NEAR * sta + half
    inside = pl.ds(PAD, rows)
    mesh_id = pl.DeviceIdType.MESH

    loads = [
        pltpu.make_async_copy(src, dst, load_sem.at[i])
        for i, (src, dst) in enumerate(
            (
                (map_hbm, map_ref),
                (slowness_hbm, slowness_ref),
                (times_ref.at[half], own_times),
                (picks_hbm, picks_ref),
                (mask_hbm, mask_ref),
            )
        )
    ]
    for load in loads:
        load.start()

    def at(other_line, other_half):
        return {"space": ((other_line + lines) % lines) * NEAR + other_half, "sta": sta}

    def member_at(other):
        return {"space": line * NEAR + other // stas, "sta": other % stas}

    barrier = pltpu.get_barrier_semaphore()

    def greet(j, carry):
        pl.semaphore_signal(
            barrier, inc=1, device_id=member_at((member + j) % members), device_id_type=mesh_id
        )
        return carry

    for other_line in (line - 1, line + 1):
        for other_half in range(NEAR):
            pl.semaphore_signal(
                barrier, inc=1, device_id=at(other_line, other_half), device_id_type=mesh_id
            )
    lax.fori_loop(1, members, greet, 0)

    rim = jnp.full((PAD, lanes), BIG, jnp.float32)

    def rims(plane, carry):
        for side in range(2):
            tab[side, plane, pl.ds(0, PAD)] = rim
            tab[side, plane, pl.ds(PAD + rows, PAD)] = rim
        return carry

    lax.fori_loop(0, count, rims, 0)

    def look_up(i, carry):
        index = map_ref[i]
        value = jnp.zeros(index.shape, jnp.float32)
        for level in range(slowness_ref.shape[0]):
            value = jnp.where(index == level, slowness_ref[level], value)
        speed_ref[i] = grid_step * value
        return carry

    loads[0].wait()
    loads[1].wait()
    lax.fori_loop(0, depth, look_up, 0)
    pl.semaphore_wait(barrier, members - 1 + 2 * NEAR)

    away = line + 2 * half - 1
    first = half * (depth - HALO)

    def start_copy(j):
        if j == 0:
            src, dst, who = times_ref.at[1 - half], swap_in, at(line, 1 - half)
        elif j == 1:
            src, dst, who = speed_ref, swap_speed, at(line, 1 - half)
        elif j < 4:
            src = times_ref.at[j - 2, pl.ds(first, HALO)]
            dst, who = halo_in.at[0, 1 - half], at(away, j - 2)
        else:
            src = speed_ref.at[pl.ds(first, HALO)]
            dst, who = halo_speed.at[1 - half], at(away, j - 4)
        slot = j if j < 2 else (2 if j < 4 else 4) + (1 - half)
        return pltpu.make_async_remote_copy(
            src_ref=src,
            dst_ref=dst,
            send_sem=start_send.at[j],
            recv_sem=start_recv.at[slot],
            device_id=who,
            device_id_type=mesh_id,
        )

    def start_arrival(slot):
        if slot == 0:
            src, dst = times_ref.at[1 - half], swap_in
        elif slot == 1:
            src, dst = speed_ref, swap_speed
        elif slot < 4:
            src, dst = times_ref.at[0, pl.ds(0, HALO)], halo_in.at[0, slot - 2]
        else:
            src, dst = speed_ref.at[pl.ds(0, HALO)], halo_speed.at[slot - 4]
        return pltpu.make_async_remote_copy(
            src_ref=src,
            dst_ref=dst,
            send_sem=start_send.at[slot],
            recv_sem=start_recv.at[slot],
            device_id=at(line, 1 - half),
            device_id_type=mesh_id,
        )

    for j in (0, 2, 3, 1, 4, 5):
        start_copy(j).start()

    at_lower = line == 0
    at_upper = line == lines - 1

    loads[3].wait()
    loads[4].wait()
    event_rows(picks_ref, mask_ref, pick_rows, mask_rows)
    spread_events(
        picks_ref.shape[0], pick_rows, mask_rows, arrival_ref, seen_ref, mean_ref, share_ref
    )
    loads[2].wait()
    for i in range(depth):
        tab[0, HALO + half * depth + i, inside] = own_times[i]
        spd[HALO + half * depth + i] = speed_ref[i]
    for slot in range(2):
        start_arrival(slot).wait_recv()
    for i in range(depth):
        tab[0, HALO + (1 - half) * depth + i, inside] = swap_in[i]
        spd[HALO + (1 - half) * depth + i] = swap_speed[i]

    def place_halo(exchange, side):
        for i in range(HALO):
            tab[side, i, inside] = jnp.where(at_lower, BIG, halo_in[exchange, 0, i])
            tab[side, HALO + own + i, inside] = jnp.where(at_upper, BIG, halo_in[exchange, 1, i])

    lane = lax.broadcasted_iota(jnp.int32, (rows, lanes), 1)

    def plane_value(side, plane, ghost):
        centre = tab[side, plane, inside]
        along_x = jnp.minimum(tab[side, plane - 1, inside], tab[side, plane + 1, inside])
        along_y = jnp.minimum(
            tab[side, plane, pl.ds(PAD - 1, rows)], tab[side, plane, pl.ds(PAD + 1, rows)]
        )
        before = jnp.where(lane == 0, BIG, pltpu.roll(centre, 1, 1))
        after = jnp.where(lane == lanes - 1, BIG, pltpu.roll(centre, lanes - 1, 1))
        along_z = jnp.minimum(before, after)
        value = jnp.minimum(centre, godunov(along_x, along_y, along_z, spd[plane]))
        if not ghost:
            return value
        outside = (at_lower & (plane < HALO)) | (at_upper & (plane >= HALO + own))
        return jnp.maximum(value, jnp.where(outside, BIG, -BIG))

    def sweep(side, total, first, store):
        def one(j, carry):
            store(first + j, plane_value(side, first + j, False))
            return carry

        unroll = next(u for u in (4, 5, 3, 2, 1) if total % u == 0)
        lax.fori_loop(0, total, one, 0, unroll=unroll)

    def sweep_edges(side, done):
        def one(j, carry):
            for plane in (done + 1 + j, HALO + own - 1 - done + j):
                tab[1 - side, plane, inside] = plane_value(side, plane, True)
            return carry

        lax.fori_loop(0, HALO, one, 0, unroll=2)

    def into(side):
        def store(plane, value):
            tab[side, plane, inside] = value

        return store

    def into_stage(plane, value):
        place = plane - HALO
        for j in range(stas):
            stage[(place // depth) * stas + j, place % depth] = value[piece * j : piece * (j + 1)]

    def into_edge(side, exchange, lower):
        def store(plane, value):
            tab[side, plane, inside] = value
            edge_out[exchange, 0 if lower else 1, plane - (HALO if lower else own)] = value

        return store

    def halo_copy(exchange, lower):
        slot = 1 if lower else 0
        return pltpu.make_async_remote_copy(
            src_ref=edge_out.at[exchange - 1, 0 if lower else 1],
            dst_ref=halo_in.at[exchange, slot],
            send_sem=halo_send.at[exchange - 1, slot],
            recv_sem=halo_recv.at[exchange - 1, slot],
            device_id=at(line - 1 if lower else line + 1, half),
            device_id_type=mesh_id,
        )

    def last_round(side, exchange):
        sweep(side, HALO, HALO, into_edge(1 - side, exchange - 1, True))
        halo_copy(exchange, True).start()
        sweep(side, HALO, own, into_edge(1 - side, exchange - 1, False))
        halo_copy(exchange, False).start()
        sweep(side, own - 2 * HALO, 2 * HALO, into(1 - side))

    exchanges = ROUNDS // HALO
    side = 0
    for exchange in range(exchanges):
        final = exchange == exchanges - 1
        start = side
        for r in range(HALO - 1):
            sweep(side, own - 2 - 2 * r, HALO + 1 + r, into(1 - side))
            side = 1 - side
        if exchange == 0:
            for slot in range(2, 6):
                start_arrival(slot).wait_recv()
            for i in range(HALO):
                spd[i] = halo_speed[0, i]
                spd[HALO + own + i] = halo_speed[1, i]
        else:
            for lower in (True, False):
                halo_copy(exchange, lower).wait()
        side = start
        place_halo(exchange, side)
        for r in range(HALO - 1):
            sweep_edges(side, r)
            side = 1 - side
        if final:
            sweep(side, own, HALO, into_stage)
        else:
            last_round(side, exchange + 1)
            side = 1 - side

    def block_copy(j):
        other = (member + j) % members
        return pltpu.make_async_remote_copy(
            src_ref=stage.at[other],
            dst_ref=arrived.at[station],
            send_sem=all_send.at[j],
            recv_sem=all_recv.at[station],
            device_id=member_at(other),
            device_id_type=mesh_id,
        )

    def block_arrival(j):
        other = (member + j) % members
        source = NEAR * (other % stas) + other // stas
        return pltpu.make_async_remote_copy(
            src_ref=stage.at[other],
            dst_ref=arrived.at[source],
            send_sem=all_send.at[j],
            recv_sem=all_recv.at[source],
            device_id=member_at(other),
            device_id_type=mesh_id,
        )

    def start_block(j, carry):
        block_copy(j).start()
        return carry

    def end_block(j, carry):
        block_copy(j).wait_send()
        block_arrival(j).wait_recv()
        return carry

    lax.fori_loop(1, members, start_block, 0)
    arrived[station] = stage[member]
    for j in range(6):
        start_copy(j).wait_send()
    lax.fori_loop(1, members, end_block, 0)
    refined_ref[...] = arrived[...]


def refined_tables(coarse_times, model_map, slowness, picks, pick_mask):
    per_device, depth, rows, lanes = coarse_times.shape
    stas = lax.axis_size("sta")
    stations = per_device * stas
    assert per_device == NEAR and ROUNDS % HALO == 0 and HALO <= depth
    piece = rows // stas
    own = NEAR * depth
    count = own + 2 * HALO
    exchanges = ROUNDS // HALO
    plane = (rows, lanes)
    vmem = pl.BlockSpec(memory_space=pltpu.VMEM)
    dma = pltpu.SemaphoreType.DMA
    events = picks.shape[0]
    wide = (events, lanes)
    hbm = pl.BlockSpec(memory_space=pltpu.HBM)
    return pl.pallas_call(
        travel_kernel,
        out_shape=(
            jax.ShapeDtypeStruct((stations, depth, piece, lanes), jnp.float32),
            jax.ShapeDtypeStruct(wide, jnp.float32),
            jax.ShapeDtypeStruct((stations,) + wide, jnp.float32),
            jax.ShapeDtypeStruct((stations,) + wide, jnp.float32),
            jax.ShapeDtypeStruct(wide, jnp.float32),
            jax.ShapeDtypeStruct(wide, jnp.float32),
        ),
        in_specs=[hbm] * 5,
        out_specs=[vmem] * 6,
        scratch_shapes=[
            pltpu.VMEM(wide, jnp.float32),
            pltpu.VMEM((depth,) + plane, jnp.float32),
            pltpu.VMEM((depth,) + plane, jnp.int32),
            pltpu.SMEM(slowness.shape, jnp.float32),
            pltpu.VMEM((stations, events), jnp.float32),
            pltpu.VMEM((stations, events), jnp.int32),
            dma((5,)),
            pltpu.VMEM((depth,) + plane, jnp.float32),
            pltpu.VMEM((2, count, rows + 2 * PAD, lanes), jnp.float32),
            pltpu.VMEM((count,) + plane, jnp.float32),
            pltpu.VMEM((depth,) + plane, jnp.float32),
            pltpu.VMEM((depth,) + plane, jnp.float32),
            pltpu.VMEM((exchanges, 2, HALO) + plane, jnp.float32),
            pltpu.VMEM((2, HALO) + plane, jnp.float32),
            pltpu.VMEM((exchanges - 1, 2, HALO) + plane, jnp.float32),
            pltpu.VMEM((NEAR * stas, depth, piece, lanes), jnp.float32),
            pltpu.VMEM((stations, depth, piece, lanes), jnp.float32),
            dma((6,)),
            dma((6,)),
            dma((exchanges - 1, 2)),
            dma((exchanges - 1, 2)),
            dma((NEAR * stas,)),
            dma((stations,)),
        ],
        compiler_params=pltpu.CompilerParams(collective_id=1, has_side_effects=True, vmem_limit_bytes=16 << 20),
        name="travel",
    )(*[pltpu.with_memory_space_constraint(x, pltpu.HBM) for x in (coarse_times, model_map, slowness, picks.T, pick_mask.T)])


def locate_kernel(
    times_ref,
    mask_rows,
    arrival_ref,
    seen_ref,
    mean_ref,
    share_ref,
    weight_ref,
    peak_ref,
    stats_ref,
    picked_sum,
    score,
    lane_mass,
    first,
    second,
    local,
    mid,
    send_sem,
    recv_sem,
):
    space = lax.axis_index("space")
    sta = lax.axis_index("sta")
    stas = lax.axis_size("sta")
    lines = lax.axis_size("space") // NEAR
    line = space // NEAR
    member = (space % NEAR) * stas + sta
    members = NEAR * stas

    def member_id(k):
        other = (member + k) % members
        return {"space": line * NEAR + other // stas, "sta": other % stas}

    def line_id(k):
        return {"space": ((line + k) % lines) * NEAR + space % NEAR, "sta": sta}

    barrier = pltpu.get_barrier_semaphore()

    def greet(ids, count):
        def one(k, carry):
            pl.semaphore_signal(barrier, inc=1, device_id=ids(k), device_id_type=pl.DeviceIdType.MESH)
            return carry

        lax.fori_loop(1, count, one, 0)

    greet(member_id, members)
    greet(line_id, lines)

    rows, events, lanes = weight_ref.shape
    stations = times_ref.shape[0] // rows
    blocks = events // lanes

    chosen = mask_rows[...].astype(jnp.bfloat16)
    blank = jnp.zeros((lanes - 3 * stations, lanes), jnp.float32)

    def pieces(row):
        part = times_ref[pl.ds(row, stations, stride=rows)]
        high = part.astype(jnp.bfloat16).astype(jnp.float32)
        rest = part - high
        middle = rest.astype(jnp.bfloat16).astype(jnp.float32)
        return jnp.concatenate([high, middle, rest - middle, blank], 0).astype(jnp.bfloat16)

    def sums(pair, carry):
        right = jnp.concatenate([pieces(2 * pair), pieces(2 * pair + 1)], 1)
        both = jnp.dot(chosen, right, preferred_element_type=jnp.float32)
        picked_sum[2 * pair] = both[:, :lanes]
        picked_sum[2 * pair + 1] = both[:, lanes:]
        return carry

    lax.fori_loop(0, rows // 2, sums, 0)

    def tile(index, carry):
        cut = pl.ds(pl.multiple_of(index * EVENT_TILE, EVENT_TILE), EVENT_TILE)
        shape = (EVENT_TILE, lanes)
        arrival = [arrival_ref[s, cut] for s in range(stations)]
        seen = [seen_ref[s, cut] for s in range(stations)]
        mean = mean_ref[cut]
        share = share_ref[cut]

        def row(r, top):
            shift = mean - picked_sum[r, cut] * share
            sums = [None] * 4
            for s in range(stations):
                time = jnp.broadcast_to(times_ref[pl.ds(s * rows + r, 1)], shape)
                deviation = (arrival[s] - time) - shift
                term = seen[s] * (deviation * deviation)
                sums[s % 4] = term if sums[s % 4] is None else sums[s % 4] + term
            misfit = functools.reduce(jnp.add, [part for part in sums if part is not None])
            value = (-0.5 / (pick_sigma * pick_sigma)) * misfit
            score[r] = value
            return jnp.maximum(top, value)

        low = jnp.full(shape, -3.0e38, jnp.float32)
        top = lax.fori_loop(0, rows, row, low, unroll=ROW_UNROLL)
        mass = jnp.zeros(shape, jnp.float32)
        for r in range(rows):
            weight = jnp.exp(score[r] - top)
            weight_ref[r, cut] = weight
            mass = mass + weight
        peak_ref[cut] = top
        lane_mass[cut] = mass
        return carry

    lax.fori_loop(0, events // EVENT_TILE, tile, 0)

    for b in range(blocks):
        cut = pl.ds(b * lanes, lanes)
        peak = peak_ref[cut].T
        top = jnp.max(peak, 0, keepdims=True)
        mass = jnp.sum(lane_mass[cut].T * jnp.exp(peak - top), 0, keepdims=True)
        local[pl.ds(b, 1)] = top
        local[pl.ds(blocks + b, 1)] = mass

    pl.semaphore_wait(barrier, members + lines - 2)

    def exchange(src, slots, ids, count, phase):
        def copy(k):
            return pltpu.make_async_remote_copy(
                src_ref=src,
                dst_ref=slots.at[k - 1],
                send_sem=send_sem.at[phase, k - 1],
                recv_sem=recv_sem.at[phase, k - 1],
                device_id=ids(k),
                device_id_type=pl.DeviceIdType.MESH,
            )

        def start(k, carry):
            copy(k).start()
            return carry

        def wait(k, carry):
            copy(k).wait()
            return carry

        lax.fori_loop(count // 4, count, start, 0)
        lax.fori_loop(1, count // 4, start, 0)
        lax.fori_loop(1, count, wait, 0)

    def merged(top, mass, slots, count):
        best = top
        for k in range(count):
            best = jnp.maximum(best, slots[k, :blocks])
        total = mass * jnp.exp(top - best)
        for k in range(count):
            total = total + slots[k, blocks:] * jnp.exp(slots[k, :blocks] - best)
        return best, total

    exchange(local, first, member_id, members, 0)
    top, mass = merged(local[:blocks], local[blocks:], first, members - 1)
    mid[:blocks] = top
    mid[blocks:] = mass
    exchange(mid, second, line_id, lines, 1)
    top, mass = merged(top, mass, second, lines - 1)
    stats_ref[:blocks] = top
    stats_ref[blocks:] = mass


def density_kernel(
    weight_ref, peak_ref, stats_ref, refined_ref, out_ref, table_ref, scale, chunk, sem, table_sem
):
    table = pltpu.make_async_copy(refined_ref, table_ref, table_sem)
    table.start()
    rows, events, lanes = weight_ref.shape
    blocks = events // lanes
    size = chunk.shape[1] // rows
    for b in range(blocks):
        cut = pl.ds(b * lanes, lanes)
        top = jnp.broadcast_to(stats_ref[pl.ds(b, 1)], (lanes, lanes)).T
        mass = jnp.broadcast_to(stats_ref[pl.ds(blocks + b, 1)], (lanes, lanes)).T
        scale[cut] = jnp.exp(peak_ref[cut] - top) / mass

    def copy(c, slot):
        return pltpu.make_async_copy(
            chunk.at[slot], out_ref.at[pl.ds(c * size * rows, size * rows)], sem.at[slot]
        )

    slots = chunk.shape[0]
    chunks = events // size
    for c in range(chunks):
        slot = c % slots
        if c >= slots:
            copy(c - slots, slot).wait()
        for t in range(size // EVENT_TILE):
            cut = pl.ds(c * size + t * EVENT_TILE, EVENT_TILE)
            factor = scale[cut]
            for r in range(rows):
                chunk[slot, pl.ds(t * EVENT_TILE * rows + r, EVENT_TILE, stride=rows)] = (
                    weight_ref[r, cut] * factor
                )
        copy(c, slot).start()
    for c in range(chunks - slots, chunks):
        copy(c, c % slots).wait()
    table.wait()


def event_density(refined, mask_rows, *events_over_lanes):
    stations, depth, piece, lanes = refined.shape
    events = mask_rows.shape[0]
    rows = depth * piece
    assert 3 * stations <= lanes and events % lanes == 0 and rows % 2 == 0
    blocks = events // lanes
    members = NEAR * lax.axis_size("sta")
    lines = lax.axis_size("space") // NEAR
    longest = max(members, lines)
    vmem = pl.BlockSpec(memory_space=pltpu.VMEM)
    wide = (events, lanes)
    message = (2 * blocks, lanes)
    f32 = jnp.float32
    weight, peak, stats = pl.pallas_call(
        locate_kernel,
        out_shape=(
            jax.ShapeDtypeStruct((rows,) + wide, f32),
            jax.ShapeDtypeStruct(wide, f32),
            jax.ShapeDtypeStruct(message, f32),
        ),
        in_specs=[vmem] * 6,
        out_specs=[vmem] * 3,
        scratch_shapes=[
            pltpu.VMEM((rows,) + wide, f32),
            pltpu.VMEM((rows, EVENT_TILE, lanes), f32),
            pltpu.VMEM(wide, f32),
            pltpu.VMEM((members - 1,) + message, f32),
            pltpu.VMEM((lines - 1,) + message, f32),
            pltpu.VMEM(message, f32),
            pltpu.VMEM(message, f32),
            pltpu.SemaphoreType.DMA((2, longest)),
            pltpu.SemaphoreType.DMA((2, longest)),
        ],
        compiler_params=pltpu.CompilerParams(collective_id=0, has_side_effects=True, vmem_limit_bytes=16 << 20),
        name="locate",
    )(refined.reshape(stations * rows, lanes), mask_rows, *events_over_lanes)
    density, table = pl.pallas_call(
        density_kernel,
        out_shape=(
            jax.ShapeDtypeStruct((events * rows, lanes), f32),
            jax.ShapeDtypeStruct(refined.shape, f32),
        ),
        in_specs=[vmem] * 4,
        out_specs=[pl.BlockSpec(memory_space=pltpu.HBM)] * 2,
        scratch_shapes=[
            pltpu.VMEM(wide, f32),
            pltpu.VMEM((4, 32 * rows, lanes), f32),
            pltpu.SemaphoreType.DMA((4,)),
            pltpu.SemaphoreType.DMA,
        ],
        compiler_params=pltpu.CompilerParams(vmem_limit_bytes=16 << 20),
        name="density",
    )(weight, peak, stats, refined)
    return table, density.reshape(events, depth, piece, lanes)


def body(coarse_times, model_map, slowness, picks, pick_mask):
    refined, *events = refined_tables(coarse_times, model_map, slowness, picks, pick_mask)
    return event_density(refined, *events)


def solution(mesh):
    placed = (P("sta", "space", None, None), P("space", None, None), P(), P(), P())
    return jax.shard_map(
        body,
        mesh=mesh,
        in_specs=placed,
        out_specs=(P(None, "space", "sta", None), P(None, "space", "sta", None)),
        check_vma=False,
    )
```

```python
import functools

import jax
import jax.numpy as jnp
from jax import lax
from jax.experimental import pallas as pl
from jax.experimental.pallas import tpu as pltpu
from jax.sharding import PartitionSpec as P

ROUNDS = 12

BIG = 1000000.0
pick_sigma = 0.25
grid_step = 1.0
NEAR = 2


BLOCKS = (4, 8)
PAD = 8
EVENT_TILE = 8
ROW_UNROLL = 5


def godunov(near_one, near_two, near_three, speed):
    small = jnp.minimum(near_one, near_two)
    large = jnp.maximum(near_one, near_two)
    lowest = jnp.minimum(small, near_three)
    highest = jnp.maximum(large, near_three)
    middle = jnp.maximum(small, jnp.minimum(large, near_three))
    gap_mid = middle - lowest
    gap_high = highest - lowest
    spread = highest - middle
    square = speed * speed
    excess = square - (gap_high * gap_high + spread * spread)
    two = excess <= 0.0
    inner = (square + square - gap_mid * gap_mid) + jnp.maximum(excess, 0.0)
    inner = jnp.maximum(inner, 1e-30)
    base = gap_mid + inner * lax.rsqrt(inner)
    steep = jnp.where(two, 0.5 * base, (base + gap_high) * (1.0 / 3.0))
    return lowest + jnp.where(speed <= gap_mid, speed, steep)


def event_rows(picks_ref, mask_ref, pick_rows, mask_rows):
    stations, events = picks_ref.shape
    lanes = pick_rows.shape[1]
    for b in range(events // lanes):
        cut = pl.ds(b * lanes, lanes)
        part = picks_ref[:, cut]
        blank = jnp.zeros((lanes - stations, lanes), jnp.float32)
        pick_rows[cut] = jnp.concatenate([part, blank], 0).T
        part = mask_ref[:, cut].astype(jnp.float32)
        blank = jnp.zeros((lanes - 3 * stations, lanes), jnp.float32)
        mask_rows[cut] = jnp.concatenate([part, part, part, blank], 0).T


def spread_events(stations, pick_rows, mask_rows, arrival_ref, seen_ref, mean_ref, share_ref):
    events, lanes = pick_rows.shape
    shape = (EVENT_TILE, lanes)

    def tile(index, carry):
        cut = pl.ds(pl.multiple_of(index * EVENT_TILE, EVENT_TILE), EVENT_TILE)
        pick = pick_rows[cut]
        mask = mask_rows[cut]
        number = None
        for s in range(stations):
            arrival = jnp.broadcast_to(pick[:, s : s + 1], shape)
            seen = jnp.broadcast_to(mask[:, s : s + 1], shape)
            arrival_ref[s, cut] = arrival
            seen_ref[s, cut] = seen
            number = seen if number is None else number + seen
            total = seen * arrival if s == 0 else total + seen * arrival
        share = 1.0 / number
        mean_ref[cut] = total * share
        share_ref[cut] = share
        return carry

    lax.fori_loop(0, events // EVENT_TILE, tile, 0)


def travel_kernel(
    times_ref,
    map_hbm,
    slowness_hbm,
    picks_hbm,
    mask_hbm,
    refined_ref,
    mask_rows,
    arrival_ref,
    seen_ref,
    mean_ref,
    share_ref,
    pick_rows,
    own_times,
    map_ref,
    slowness_ref,
    picks_ref,
    mask_ref,
    load_sem,
    speed_ref,
    tab,
    spd,
    swap_in,
    swap_speed,
    halo_first,
    halo_next,
    near_speed,
    rest_speed,
    far_speed,
    edge_out,
    stage,
    arrived,
    start_send,
    start_recv,
    halo_send,
    halo_recv,
    all_send,
    all_recv,
):
    space = lax.axis_index("space")
    sta = lax.axis_index("sta")
    stas = lax.axis_size("sta")
    lines = lax.axis_size("space") // NEAR
    line = space // NEAR
    half = space % NEAR
    depth, rows, lanes = map_ref.shape
    own = NEAR * depth
    near, ghost = BLOCKS
    far = ghost - depth
    count = own + 2 * ghost
    piece = stage.shape[2]
    member = half * stas + sta
    members = NEAR * stas
    station = NEAR * sta + half
    inside = pl.ds(PAD, rows)
    mesh_id = pl.DeviceIdType.MESH

    loads = [
        pltpu.make_async_copy(src, dst, load_sem.at[i])
        for i, (src, dst) in enumerate(
            (
                (map_hbm, map_ref),
                (slowness_hbm, slowness_ref),
                (times_ref.at[half], own_times),
                (picks_hbm, picks_ref),
                (mask_hbm, mask_ref),
            )
        )
    ]
    for load in loads:
        load.start()

    def at(other_line, other_half):
        return {"space": ((other_line + lines) % lines) * NEAR + other_half, "sta": sta}

    def member_at(other):
        return {"space": line * NEAR + other // stas, "sta": other % stas}

    barrier = pltpu.get_barrier_semaphore()

    def greet(j, carry):
        pl.semaphore_signal(
            barrier, inc=1, device_id=member_at((member + j) % members), device_id_type=mesh_id
        )
        return carry

    for other_line in (line - 1, line + 1):
        for other_half in range(NEAR):
            pl.semaphore_signal(
                barrier, inc=1, device_id=at(other_line, other_half), device_id_type=mesh_id
            )
    lax.fori_loop(1, members, greet, 0)

    rim = jnp.full((PAD, lanes), BIG, jnp.float32)

    def rims(plane, carry):
        for side in range(2):
            tab[side, plane, pl.ds(0, PAD)] = rim
            tab[side, plane, pl.ds(PAD + rows, PAD)] = rim
        return carry

    lax.fori_loop(0, count, rims, 0)

    def look_up(i, carry):
        index = map_ref[i]
        value = jnp.zeros(index.shape, jnp.float32)
        for level in range(slowness_ref.shape[0]):
            value = jnp.where(index == level, slowness_ref[level], value)
        speed_ref[i] = grid_step * value
        return carry

    loads[0].wait()
    loads[1].wait()
    lax.fori_loop(0, depth, look_up, 0)
    pl.semaphore_wait(barrier, members - 1 + 2 * NEAR)

    away = line + 2 * half - 1
    back = line - 2 * half + 1

    def start_copy(j):
        kind, other = j // 2, j % 2
        if kind == 0:
            src, dst = ((times_ref.at[1 - half], swap_in), (speed_ref, swap_speed))[other]
            who, slot = at(line, 1 - half), other
        elif kind == 1:
            src = times_ref.at[other, pl.ds(half * (depth - near), near)]
            dst, who, slot = halo_first.at[1 - half], at(away, other), 2 + (1 - half)
        elif kind == 2:
            src = speed_ref.at[pl.ds(half * (depth - near), near)]
            dst, who, slot = near_speed.at[1 - half], at(away, other), 4 + (1 - half)
        elif kind == 3:
            src = speed_ref.at[pl.ds((1 - half) * near, depth - near)]
            dst, who, slot = rest_speed.at[1 - half], at(away, other), 6 + (1 - half)
        else:
            src = speed_ref.at[pl.ds((1 - half) * (depth - far), far)]
            dst, who, slot = far_speed.at[half], at(back, other), 8 + half
        return pltpu.make_async_remote_copy(
            src_ref=src,
            dst_ref=dst,
            send_sem=start_send.at[j],
            recv_sem=start_recv.at[slot],
            device_id=who,
            device_id_type=mesh_id,
        )

    def start_arrival(slot):
        kind, other = slot // 2, slot % 2
        src, dst = (
            ((times_ref.at[0], swap_in), (speed_ref, swap_speed))[other],
            (times_ref.at[0, pl.ds(0, near)], halo_first.at[other]),
            (speed_ref.at[pl.ds(0, near)], near_speed.at[other]),
            (speed_ref.at[pl.ds(0, depth - near)], rest_speed.at[other]),
            (speed_ref.at[pl.ds(0, far)], far_speed.at[other]),
        )[kind]
        return pltpu.make_async_remote_copy(
            src_ref=src,
            dst_ref=dst,
            send_sem=start_send.at[slot],
            recv_sem=start_recv.at[slot],
            device_id=at(line, 1 - half),
            device_id_type=mesh_id,
        )

    for j in (0, 2, 3, 1, 4, 5, 6, 7, 8, 9):
        start_copy(j).start()

    at_lower = line == 0
    at_upper = line == lines - 1

    loads[3].wait()
    loads[4].wait()
    event_rows(picks_ref, mask_ref, pick_rows, mask_rows)
    spread_events(
        picks_ref.shape[0], pick_rows, mask_rows, arrival_ref, seen_ref, mean_ref, share_ref
    )
    loads[2].wait()
    for i in range(depth):
        tab[0, ghost + half * depth + i, inside] = own_times[i]
        spd[ghost + half * depth + i] = speed_ref[i]
    for slot in range(2):
        start_arrival(slot).wait_recv()
    for i in range(depth):
        tab[0, ghost + (1 - half) * depth + i, inside] = swap_in[i]
        spd[ghost + (1 - half) * depth + i] = swap_speed[i]

    def place_halo(arrived_planes, width, side):
        for i in range(width):
            below, above = ghost - width + i, ghost + own + i
            tab[side, below, inside] = jnp.where(at_lower, BIG, arrived_planes[0, i])
            tab[side, above, inside] = jnp.where(at_upper, BIG, arrived_planes[1, i])

    lane = lax.broadcasted_iota(jnp.int32, (rows, lanes), 1)

    def plane_value(side, plane, rim):
        centre = tab[side, plane, inside]
        along_x = jnp.minimum(tab[side, plane - 1, inside], tab[side, plane + 1, inside])
        along_y = jnp.minimum(
            tab[side, plane, pl.ds(PAD - 1, rows)], tab[side, plane, pl.ds(PAD + 1, rows)]
        )
        before = jnp.where(lane == 0, BIG, pltpu.roll(centre, 1, 1))
        after = jnp.where(lane == lanes - 1, BIG, pltpu.roll(centre, lanes - 1, 1))
        along_z = jnp.minimum(before, after)
        value = jnp.minimum(centre, godunov(along_x, along_y, along_z, spd[plane]))
        if not rim:
            return value
        outside = (at_lower & (plane < ghost)) | (at_upper & (plane >= ghost + own))
        return jnp.maximum(value, jnp.where(outside, BIG, -BIG))

    def sweep(side, total, first, store, rim=False):
        def one(j, carry):
            store(first + j, plane_value(side, first + j, rim))
            return carry

        unroll = next(u for u in (4, 5, 3, 2, 1) if total % u == 0)
        lax.fori_loop(0, total, one, 0, unroll=unroll)

    def sweep_edges(side, done, width):
        def one(j, carry):
            for plane in (ghost - width + 1 + done + j, ghost + own - 1 - done + j):
                tab[1 - side, plane, inside] = plane_value(side, plane, True)
            return carry

        lax.fori_loop(0, width, one, 0, unroll=2)

    def into(side):
        def store(plane, value):
            tab[side, plane, inside] = value

        return store

    def into_stage(plane, value):
        place = plane - ghost
        for j in range(stas):
            stage[(place // depth) * stas + j, place % depth] = value[piece * j : piece * (j + 1)]

    def into_edge(side):
        def store(plane, value):
            tab[side, plane, inside] = value
            edge_out[plane - ghost] = value

        return store

    def halo_copy(lower):
        slot = 1 if lower else 0
        return pltpu.make_async_remote_copy(
            src_ref=edge_out.at[pl.ds(0 if lower else own - ghost, ghost)],
            dst_ref=halo_next.at[slot],
            send_sem=halo_send.at[slot],
            recv_sem=halo_recv.at[slot],
            device_id=at(line - 1 if lower else line + 1, half),
            device_id_type=mesh_id,
        )

    side = 0
    for block, width in enumerate(BLOCKS):
        start = side
        for r in range(width - 1):
            if own - 2 - 2 * r > 0:
                sweep(side, own - 2 - 2 * r, ghost + 1 + r, into(1 - side))
                side = 1 - side
        if block == 0:
            for slot in range(2, 6):
                start_arrival(slot).wait_recv()
            for i in range(near):
                spd[ghost - near + i] = near_speed[0, i]
                spd[ghost + own + i] = near_speed[1, i]
        else:
            for slot in range(6, 10):
                start_arrival(slot).wait_recv()
            for i in range(depth - near):
                spd[far + i] = rest_speed[0, i]
                spd[ghost + own + near + i] = rest_speed[1, i]
            for i in range(far):
                spd[i] = far_speed[0, i]
                spd[ghost + own + depth + i] = far_speed[1, i]
            for lower in (True, False):
                halo_copy(lower).wait()
        side = start
        place_halo(halo_first if block == 0 else halo_next, width, side)
        for r in range(width - 1):
            if own - 2 - 2 * r >= 0:
                sweep_edges(side, r, width)
            else:
                total = own + 2 * (width - 1 - r)
                sweep(side, total, ghost - width + 1 + r, into(1 - side), True)
            side = 1 - side
        if block == 0:
            sweep(side, own, ghost, into_edge(1 - side))
            for lower in (True, False):
                halo_copy(lower).start()
            side = 1 - side
        else:
            sweep(side, own, ghost, into_stage)

    def block_copy(j):
        other = (member + j) % members
        return pltpu.make_async_remote_copy(
            src_ref=stage.at[other],
            dst_ref=arrived.at[station],
            send_sem=all_send.at[j],
            recv_sem=all_recv.at[station],
            device_id=member_at(other),
            device_id_type=mesh_id,
        )

    def block_arrival(j):
        other = (member + j) % members
        source = NEAR * (other % stas) + other // stas
        return pltpu.make_async_remote_copy(
            src_ref=stage.at[other],
            dst_ref=arrived.at[source],
            send_sem=all_send.at[j],
            recv_sem=all_recv.at[source],
            device_id=member_at(other),
            device_id_type=mesh_id,
        )

    def start_block(j, carry):
        block_copy(j).start()
        return carry

    def end_block(j, carry):
        block_copy(j).wait_send()
        block_arrival(j).wait_recv()
        return carry

    lax.fori_loop(1, members, start_block, 0)
    arrived[station] = stage[member]
    for j in range(10):
        start_copy(j).wait_send()
    lax.fori_loop(1, members, end_block, 0)
    refined_ref[...] = arrived[...]


def refined_tables(coarse_times, model_map, slowness, picks, pick_mask):
    per_device, depth, rows, lanes = coarse_times.shape
    stas = lax.axis_size("sta")
    stations = per_device * stas
    near, ghost = BLOCKS
    own = NEAR * depth
    assert per_device == NEAR and sum(BLOCKS) == ROUNDS and near < depth < ghost <= own
    piece = rows // stas
    count = own + 2 * ghost
    plane = (rows, lanes)
    vmem = pl.BlockSpec(memory_space=pltpu.VMEM)
    dma = pltpu.SemaphoreType.DMA
    events = picks.shape[0]
    wide = (events, lanes)
    hbm = pl.BlockSpec(memory_space=pltpu.HBM)
    return pl.pallas_call(
        travel_kernel,
        out_shape=(
            jax.ShapeDtypeStruct((stations, depth, piece, lanes), jnp.float32),
            jax.ShapeDtypeStruct(wide, jnp.float32),
            jax.ShapeDtypeStruct((stations,) + wide, jnp.float32),
            jax.ShapeDtypeStruct((stations,) + wide, jnp.float32),
            jax.ShapeDtypeStruct(wide, jnp.float32),
            jax.ShapeDtypeStruct(wide, jnp.float32),
        ),
        in_specs=[hbm] * 5,
        out_specs=[vmem] * 6,
        scratch_shapes=[
            pltpu.VMEM(wide, jnp.float32),
            pltpu.VMEM((depth,) + plane, jnp.float32),
            pltpu.VMEM((depth,) + plane, jnp.int32),
            pltpu.SMEM(slowness.shape, jnp.float32),
            pltpu.VMEM((stations, events), jnp.float32),
            pltpu.VMEM((stations, events), jnp.int32),
            dma((5,)),
            pltpu.VMEM((depth,) + plane, jnp.float32),
            pltpu.VMEM((2, count, rows + 2 * PAD, lanes), jnp.float32),
            pltpu.VMEM((count,) + plane, jnp.float32),
            pltpu.VMEM((depth,) + plane, jnp.float32),
            pltpu.VMEM((depth,) + plane, jnp.float32),
            pltpu.VMEM((2, near) + plane, jnp.float32),
            pltpu.VMEM((2, ghost) + plane, jnp.float32),
            pltpu.VMEM((2, near) + plane, jnp.float32),
            pltpu.VMEM((2, depth - near) + plane, jnp.float32),
            pltpu.VMEM((2, ghost - depth) + plane, jnp.float32),
            pltpu.VMEM((own,) + plane, jnp.float32),
            pltpu.VMEM((NEAR * stas, depth, piece, lanes), jnp.float32),
            pltpu.VMEM((stations, depth, piece, lanes), jnp.float32),
            dma((10,)),
            dma((10,)),
            dma((2,)),
            dma((2,)),
            dma((NEAR * stas,)),
            dma((stations,)),
        ],
        compiler_params=pltpu.CompilerParams(collective_id=1, has_side_effects=True, vmem_limit_bytes=16 << 20),
        name="travel",
    )(*[pltpu.with_memory_space_constraint(x, pltpu.HBM) for x in (coarse_times, model_map, slowness, picks.T, pick_mask.T)])


def locate_kernel(
    times_ref,
    mask_rows,
    arrival_ref,
    seen_ref,
    mean_ref,
    share_ref,
    weight_ref,
    peak_ref,
    stats_ref,
    picked_sum,
    score,
    lane_mass,
    first,
    second,
    local,
    mid,
    send_sem,
    recv_sem,
):
    space = lax.axis_index("space")
    sta = lax.axis_index("sta")
    stas = lax.axis_size("sta")
    lines = lax.axis_size("space") // NEAR
    line = space // NEAR
    member = (space % NEAR) * stas + sta
    members = NEAR * stas

    def member_id(k):
        other = (member + k) % members
        return {"space": line * NEAR + other // stas, "sta": other % stas}

    def line_id(k):
        return {"space": ((line + k) % lines) * NEAR + space % NEAR, "sta": sta}

    barrier = pltpu.get_barrier_semaphore()

    def greet(ids, count):
        def one(k, carry):
            pl.semaphore_signal(barrier, inc=1, device_id=ids(k), device_id_type=pl.DeviceIdType.MESH)
            return carry

        lax.fori_loop(1, count, one, 0)

    greet(member_id, members)
    greet(line_id, lines)

    rows, events, lanes = weight_ref.shape
    stations = times_ref.shape[0] // rows
    blocks = events // lanes

    chosen = mask_rows[...].astype(jnp.bfloat16)
    blank = jnp.zeros((lanes - 3 * stations, lanes), jnp.float32)

    def pieces(row):
        part = times_ref[pl.ds(row, stations, stride=rows)]
        high = part.astype(jnp.bfloat16).astype(jnp.float32)
        rest = part - high
        middle = rest.astype(jnp.bfloat16).astype(jnp.float32)
        return jnp.concatenate([high, middle, rest - middle, blank], 0).astype(jnp.bfloat16)

    def sums(pair, carry):
        right = jnp.concatenate([pieces(2 * pair), pieces(2 * pair + 1)], 1)
        both = jnp.dot(chosen, right, preferred_element_type=jnp.float32)
        picked_sum[2 * pair] = both[:, :lanes]
        picked_sum[2 * pair + 1] = both[:, lanes:]
        return carry

    lax.fori_loop(0, rows // 2, sums, 0)

    def tile(index, carry):
        cut = pl.ds(pl.multiple_of(index * EVENT_TILE, EVENT_TILE), EVENT_TILE)
        shape = (EVENT_TILE, lanes)
        arrival = [arrival_ref[s, cut] for s in range(stations)]
        seen = [seen_ref[s, cut] for s in range(stations)]
        mean = mean_ref[cut]
        share = share_ref[cut]

        def row(r, top):
            shift = mean - picked_sum[r, cut] * share
            sums = [None] * 4
            for s in range(stations):
                time = jnp.broadcast_to(times_ref[pl.ds(s * rows + r, 1)], shape)
                deviation = (arrival[s] - time) - shift
                term = seen[s] * (deviation * deviation)
                sums[s % 4] = term if sums[s % 4] is None else sums[s % 4] + term
            misfit = functools.reduce(jnp.add, [part for part in sums if part is not None])
            value = (-0.5 / (pick_sigma * pick_sigma)) * misfit
            score[r] = value
            return jnp.maximum(top, value)

        low = jnp.full(shape, -3.0e38, jnp.float32)
        top = lax.fori_loop(0, rows, row, low, unroll=ROW_UNROLL)
        mass = jnp.zeros(shape, jnp.float32)
        for r in range(rows):
            weight = jnp.exp(score[r] - top)
            weight_ref[r, cut] = weight
            mass = mass + weight
        peak_ref[cut] = top
        lane_mass[cut] = mass
        return carry

    lax.fori_loop(0, events // EVENT_TILE, tile, 0)

    for b in range(blocks):
        cut = pl.ds(b * lanes, lanes)
        peak = peak_ref[cut].T
        top = jnp.max(peak, 0, keepdims=True)
        mass = jnp.sum(lane_mass[cut].T * jnp.exp(peak - top), 0, keepdims=True)
        local[pl.ds(b, 1)] = top
        local[pl.ds(blocks + b, 1)] = mass

    pl.semaphore_wait(barrier, members + lines - 2)

    def exchange(src, slots, ids, count, phase):
        def copy(k):
            return pltpu.make_async_remote_copy(
                src_ref=src,
                dst_ref=slots.at[k - 1],
                send_sem=send_sem.at[phase, k - 1],
                recv_sem=recv_sem.at[phase, k - 1],
                device_id=ids(k),
                device_id_type=pl.DeviceIdType.MESH,
            )

        def start(k, carry):
            copy(k).start()
            return carry

        def wait(k, carry):
            copy(k).wait()
            return carry

        lax.fori_loop(count // 4, count, start, 0)
        lax.fori_loop(1, count // 4, start, 0)
        lax.fori_loop(1, count, wait, 0)

    def merged(top, mass, slots, count):
        best = top
        for k in range(count):
            best = jnp.maximum(best, slots[k, :blocks])
        total = mass * jnp.exp(top - best)
        for k in range(count):
            total = total + slots[k, blocks:] * jnp.exp(slots[k, :blocks] - best)
        return best, total

    exchange(local, first, member_id, members, 0)
    top, mass = merged(local[:blocks], local[blocks:], first, members - 1)
    mid[:blocks] = top
    mid[blocks:] = mass
    exchange(mid, second, line_id, lines, 1)
    top, mass = merged(top, mass, second, lines - 1)
    stats_ref[:blocks] = top
    stats_ref[blocks:] = mass


def density_kernel(
    weight_ref, peak_ref, stats_ref, refined_ref, out_ref, table_ref, scale, chunk, sem, table_sem
):
    table = pltpu.make_async_copy(refined_ref, table_ref, table_sem)
    table.start()
    rows, events, lanes = weight_ref.shape
    blocks = events // lanes
    size = chunk.shape[1] // rows
    for b in range(blocks):
        cut = pl.ds(b * lanes, lanes)
        top = jnp.broadcast_to(stats_ref[pl.ds(b, 1)], (lanes, lanes)).T
        mass = jnp.broadcast_to(stats_ref[pl.ds(blocks + b, 1)], (lanes, lanes)).T
        scale[cut] = jnp.exp(peak_ref[cut] - top) / mass

    def copy(c, slot):
        return pltpu.make_async_copy(
            chunk.at[slot], out_ref.at[pl.ds(c * size * rows, size * rows)], sem.at[slot]
        )

    slots = chunk.shape[0]
    chunks = events // size
    for c in range(chunks):
        slot = c % slots
        if c >= slots:
            copy(c - slots, slot).wait()
        for t in range(size // EVENT_TILE):
            cut = pl.ds(c * size + t * EVENT_TILE, EVENT_TILE)
            factor = scale[cut]
            for r in range(rows):
                chunk[slot, pl.ds(t * EVENT_TILE * rows + r, EVENT_TILE, stride=rows)] = (
                    weight_ref[r, cut] * factor
                )
        copy(c, slot).start()
    for c in range(chunks - slots, chunks):
        copy(c, c % slots).wait()
    table.wait()


def event_density(refined, mask_rows, *events_over_lanes):
    stations, depth, piece, lanes = refined.shape
    events = mask_rows.shape[0]
    rows = depth * piece
    assert 3 * stations <= lanes and events % lanes == 0 and rows % 2 == 0
    blocks = events // lanes
    members = NEAR * lax.axis_size("sta")
    lines = lax.axis_size("space") // NEAR
    longest = max(members, lines)
    vmem = pl.BlockSpec(memory_space=pltpu.VMEM)
    wide = (events, lanes)
    message = (2 * blocks, lanes)
    f32 = jnp.float32
    weight, peak, stats = pl.pallas_call(
        locate_kernel,
        out_shape=(
            jax.ShapeDtypeStruct((rows,) + wide, f32),
            jax.ShapeDtypeStruct(wide, f32),
            jax.ShapeDtypeStruct(message, f32),
        ),
        in_specs=[vmem] * 6,
        out_specs=[vmem] * 3,
        scratch_shapes=[
            pltpu.VMEM((rows,) + wide, f32),
            pltpu.VMEM((rows, EVENT_TILE, lanes), f32),
            pltpu.VMEM(wide, f32),
            pltpu.VMEM((members - 1,) + message, f32),
            pltpu.VMEM((lines - 1,) + message, f32),
            pltpu.VMEM(message, f32),
            pltpu.VMEM(message, f32),
            pltpu.SemaphoreType.DMA((2, longest)),
            pltpu.SemaphoreType.DMA((2, longest)),
        ],
        compiler_params=pltpu.CompilerParams(collective_id=0, has_side_effects=True, vmem_limit_bytes=16 << 20),
        name="locate",
    )(refined.reshape(stations * rows, lanes), mask_rows, *events_over_lanes)
    density, table = pl.pallas_call(
        density_kernel,
        out_shape=(
            jax.ShapeDtypeStruct((events * rows, lanes), f32),
            jax.ShapeDtypeStruct(refined.shape, f32),
        ),
        in_specs=[vmem] * 4,
        out_specs=[pl.BlockSpec(memory_space=pltpu.HBM)] * 2,
        scratch_shapes=[
            pltpu.VMEM(wide, f32),
            pltpu.VMEM((4, 32 * rows, lanes), f32),
            pltpu.SemaphoreType.DMA((4,)),
            pltpu.SemaphoreType.DMA,
        ],
        compiler_params=pltpu.CompilerParams(vmem_limit_bytes=16 << 20),
        name="density",
    )(weight, peak, stats, refined)
    return table, density.reshape(events, depth, piece, lanes)


def body(coarse_times, model_map, slowness, picks, pick_mask):
    refined, *events = refined_tables(coarse_times, model_map, slowness, picks, pick_mask)
    return event_density(refined, *events)


def solution(mesh):
    placed = (P("sta", "space", None, None), P("space", None, None), P(), P(), P())
    return jax.shard_map(
        body,
        mesh=mesh,
        in_specs=placed,
        out_specs=(P(None, "space", "sta", None), P(None, "space", "sta", None)),
        check_vma=False,
    )
```

```python
import functools

import jax
import jax.numpy as jnp
from jax import lax
from jax.experimental import pallas as pl
from jax.experimental.pallas import tpu as pltpu
from jax.sharding import PartitionSpec as P

ROUNDS = 12

BIG = 1000000.0
pick_sigma = 0.25
grid_step = 1.0
NEAR = 2


BLOCKS = (4, 8)
PAD = 8
EVENT_TILE = 8
ROW_UNROLL = 5


def godunov(near_one, near_two, near_three, speed):
    small = jnp.minimum(near_one, near_two)
    large = jnp.maximum(near_one, near_two)
    lowest = jnp.minimum(small, near_three)
    highest = jnp.maximum(large, near_three)
    middle = jnp.maximum(small, jnp.minimum(large, near_three))
    gap_mid = middle - lowest
    gap_high = highest - lowest
    spread = highest - middle
    square = speed * speed
    excess = square - (gap_high * gap_high + spread * spread)
    two = excess <= 0.0
    inner = (square + square - gap_mid * gap_mid) + jnp.maximum(excess, 0.0)
    inner = jnp.maximum(inner, 1e-30)
    base = gap_mid + inner * lax.rsqrt(inner)
    steep = jnp.where(two, 0.5 * base, (base + gap_high) * (1.0 / 3.0))
    return lowest + jnp.where(speed <= gap_mid, speed, steep)


def event_rows(picks_ref, mask_ref, pick_rows, mask_rows):
    stations, events = picks_ref.shape
    lanes = pick_rows.shape[1]
    for b in range(events // lanes):
        cut = pl.ds(b * lanes, lanes)
        part = picks_ref[:, cut]
        blank = jnp.zeros((lanes - stations, lanes), jnp.float32)
        pick_rows[cut] = jnp.concatenate([part, blank], 0).T
        part = mask_ref[:, cut].astype(jnp.float32)
        blank = jnp.zeros((lanes - 3 * stations, lanes), jnp.float32)
        mask_rows[cut] = jnp.concatenate([part, part, part, blank], 0).T


def spread_events(stations, pick_rows, mask_rows, arrival_ref, seen_ref, mean_ref, share_ref):
    events, lanes = pick_rows.shape
    shape = (EVENT_TILE, lanes)

    def tile(index, carry):
        cut = pl.ds(pl.multiple_of(index * EVENT_TILE, EVENT_TILE), EVENT_TILE)
        pick = pick_rows[cut]
        mask = mask_rows[cut]
        number = None
        for s in range(stations):
            arrival = jnp.broadcast_to(pick[:, s : s + 1], shape)
            seen = jnp.broadcast_to(mask[:, s : s + 1], shape)
            arrival_ref[s, cut] = arrival
            seen_ref[s, cut] = seen
            number = seen if number is None else number + seen
            total = seen * arrival if s == 0 else total + seen * arrival
        share = 1.0 / number
        mean_ref[cut] = total * share
        share_ref[cut] = share
        return carry

    lax.fori_loop(0, events // EVENT_TILE, tile, 0)


def travel_kernel(
    times_ref,
    map_hbm,
    slowness_hbm,
    picks_hbm,
    mask_hbm,
    refined_ref,
    mask_rows,
    arrival_ref,
    seen_ref,
    mean_ref,
    share_ref,
    pick_rows,
    own_times,
    map_ref,
    slowness_ref,
    picks_ref,
    mask_ref,
    load_sem,
    speed_ref,
    tab,
    spd,
    swap_in,
    swap_speed,
    halo_first,
    halo_next,
    near_speed,
    rest_speed,
    far_speed,
    edge_out,
    stage,
    arrived,
    start_send,
    start_recv,
    halo_send,
    halo_recv,
    all_send,
    all_recv,
):
    space = lax.axis_index("space")
    sta = lax.axis_index("sta")
    stas = lax.axis_size("sta")
    lines = lax.axis_size("space") // NEAR
    line = lax.div(space, NEAR)
    half = lax.rem(space, NEAR)
    depth, rows, lanes = map_ref.shape
    own = NEAR * depth
    near, ghost = BLOCKS
    far = ghost - depth
    count = own + 2 * ghost
    piece = stage.shape[2]
    member = half * stas + sta
    members = NEAR * stas
    station = NEAR * sta + half
    inside = pl.ds(PAD, rows)
    mesh_id = pl.DeviceIdType.MESH

    loads = [
        pltpu.make_async_copy(src, dst, load_sem.at[i])
        for i, (src, dst) in enumerate(
            (
                (map_hbm, map_ref),
                (slowness_hbm, slowness_ref),
                (times_ref.at[half], own_times),
                (picks_hbm, picks_ref),
                (mask_hbm, mask_ref),
            )
        )
    ]
    for load in loads:
        load.start()

    def at(other_line, other_half):
        return {"space": lax.rem(other_line + lines, lines) * NEAR + other_half, "sta": sta}

    def member_at(other):
        return {"space": line * NEAR + lax.div(other, stas), "sta": lax.rem(other, stas)}

    barrier = pltpu.get_barrier_semaphore()

    def greet(j, carry):
        pl.semaphore_signal(
            barrier, inc=1, device_id=member_at(lax.rem(member + j, members)), device_id_type=mesh_id
        )
        return carry

    for other_line in (line - 1, line + 1):
        for other_half in range(NEAR):
            pl.semaphore_signal(
                barrier, inc=1, device_id=at(other_line, other_half), device_id_type=mesh_id
            )
    lax.fori_loop(1, members, greet, 0)

    rim = jnp.full((PAD, lanes), BIG, jnp.float32)

    def rims(plane, carry):
        for side in range(2):
            tab[side, plane, pl.ds(0, PAD)] = rim
            tab[side, plane, pl.ds(PAD + rows, PAD)] = rim
        return carry

    lax.fori_loop(0, count, rims, 0)

    def look_up(i, carry):
        index = map_ref[i]
        value = jnp.zeros(index.shape, jnp.float32)
        for level in range(slowness_ref.shape[0]):
            value = jnp.where(index == level, slowness_ref[level], value)
        speed_ref[i] = grid_step * value
        return carry

    loads[0].wait()
    loads[1].wait()
    lax.fori_loop(0, depth, look_up, 0)
    pl.semaphore_wait(barrier, members - 1 + 2 * NEAR)

    away = line + 2 * half - 1
    back = line - 2 * half + 1

    def start_copy(j):
        kind, other = j // 2, j % 2
        if kind == 0:
            src, dst = ((times_ref.at[1 - half], swap_in), (speed_ref, swap_speed))[other]
            who, slot = at(line, 1 - half), other
        elif kind == 1:
            src = times_ref.at[other, pl.ds(half * (depth - near), near)]
            dst, who, slot = halo_first.at[1 - half], at(away, other), 2 + (1 - half)
        elif kind == 2:
            src = speed_ref.at[pl.ds(half * (depth - near), near)]
            dst, who, slot = near_speed.at[1 - half], at(away, other), 4 + (1 - half)
        elif kind == 3:
            src = speed_ref.at[pl.ds((1 - half) * near, depth - near)]
            dst, who, slot = rest_speed.at[1 - half], at(away, other), 6 + (1 - half)
        else:
            src = speed_ref.at[pl.ds((1 - half) * (depth - far), far)]
            dst, who, slot = far_speed.at[half], at(back, other), 8 + half
        return pltpu.make_async_remote_copy(
            src_ref=src,
            dst_ref=dst,
            send_sem=start_send.at[j],
            recv_sem=start_recv.at[slot],
            device_id=who,
            device_id_type=mesh_id,
        )

    def start_arrival(slot):
        kind, other = slot // 2, slot % 2
        src, dst = (
            ((times_ref.at[0], swap_in), (speed_ref, swap_speed))[other],
            (times_ref.at[0, pl.ds(0, near)], halo_first.at[other]),
            (speed_ref.at[pl.ds(0, near)], near_speed.at[other]),
            (speed_ref.at[pl.ds(0, depth - near)], rest_speed.at[other]),
            (speed_ref.at[pl.ds(0, far)], far_speed.at[other]),
        )[kind]
        return pltpu.make_async_remote_copy(
            src_ref=src,
            dst_ref=dst,
            send_sem=start_send.at[slot],
            recv_sem=start_recv.at[slot],
            device_id=at(line, 1 - half),
            device_id_type=mesh_id,
        )

    for j in (0, 2, 3, 1, 4, 5, 6, 7, 8, 9):
        start_copy(j).start()

    at_lower = line == 0
    at_upper = line == lines - 1

    loads[3].wait()
    loads[4].wait()
    event_rows(picks_ref, mask_ref, pick_rows, mask_rows)
    spread_events(
        picks_ref.shape[0], pick_rows, mask_rows, arrival_ref, seen_ref, mean_ref, share_ref
    )
    loads[2].wait()
    for i in range(depth):
        tab[0, ghost + half * depth + i, inside] = own_times[i]
        spd[ghost + half * depth + i] = speed_ref[i]
    for slot in range(2):
        start_arrival(slot).wait_recv()
    for i in range(depth):
        tab[0, ghost + (1 - half) * depth + i, inside] = swap_in[i]
        spd[ghost + (1 - half) * depth + i] = swap_speed[i]

    def place_halo(arrived_planes, width, side):
        for i in range(width):
            below, above = ghost - width + i, ghost + own + i
            tab[side, below, inside] = jnp.where(at_lower, BIG, arrived_planes[0, i])
            tab[side, above, inside] = jnp.where(at_upper, BIG, arrived_planes[1, i])

    lane = lax.broadcasted_iota(jnp.int32, (rows, lanes), 1)

    def plane_value(side, plane, rim):
        centre = tab[side, plane, inside]
        along_x = jnp.minimum(tab[side, plane - 1, inside], tab[side, plane + 1, inside])
        along_y = jnp.minimum(
            tab[side, plane, pl.ds(PAD - 1, rows)], tab[side, plane, pl.ds(PAD + 1, rows)]
        )
        before = jnp.where(lane == 0, BIG, pltpu.roll(centre, 1, 1))
        after = jnp.where(lane == lanes - 1, BIG, pltpu.roll(centre, lanes - 1, 1))
        along_z = jnp.minimum(before, after)
        value = jnp.minimum(centre, godunov(along_x, along_y, along_z, spd[plane]))
        if not rim:
            return value
        outside = (at_lower & (plane < ghost)) | (at_upper & (plane >= ghost + own))
        return jnp.maximum(value, jnp.where(outside, BIG, -BIG))

    def sweep(side, total, first, store, rim=False):
        def one(j, carry):
            store(first + j, plane_value(side, first + j, rim))
            return carry

        unroll = next(u for u in (4, 5, 3, 2, 1) if total % u == 0)
        lax.fori_loop(0, total, one, 0, unroll=unroll)

    def sweep_edges(side, done, width):
        def one(j, carry):
            for plane in (ghost - width + 1 + done + j, ghost + own - 1 - done + j):
                tab[1 - side, plane, inside] = plane_value(side, plane, True)
            return carry

        lax.fori_loop(0, width, one, 0, unroll=2)

    def into(side):
        def store(plane, value):
            tab[side, plane, inside] = value

        return store

    def into_stage(plane, value):
        place = plane - ghost
        for j in range(stas):
            stage[(lax.div(place, depth)) * stas + j, lax.rem(place, depth)] = value[piece * j : piece * (j + 1)]

    def into_edge(side):
        def store(plane, value):
            tab[side, plane, inside] = value
            edge_out[plane - ghost] = value

        return store

    def halo_copy(lower):
        slot = 1 if lower else 0
        return pltpu.make_async_remote_copy(
            src_ref=edge_out.at[pl.ds(0 if lower else own - ghost, ghost)],
            dst_ref=halo_next.at[slot],
            send_sem=halo_send.at[slot],
            recv_sem=halo_recv.at[slot],
            device_id=at(line - 1 if lower else line + 1, half),
            device_id_type=mesh_id,
        )

    side = 0
    for block, width in enumerate(BLOCKS):
        start = side
        for r in range(width - 1):
            if own - 2 - 2 * r > 0:
                sweep(side, own - 2 - 2 * r, ghost + 1 + r, into(1 - side))
                side = 1 - side
        if block == 0:
            for slot in range(2, 6):
                start_arrival(slot).wait_recv()
            for i in range(near):
                spd[ghost - near + i] = near_speed[0, i]
                spd[ghost + own + i] = near_speed[1, i]
        else:
            for slot in range(6, 10):
                start_arrival(slot).wait_recv()
            for i in range(depth - near):
                spd[far + i] = rest_speed[0, i]
                spd[ghost + own + near + i] = rest_speed[1, i]
            for i in range(far):
                spd[i] = far_speed[0, i]
                spd[ghost + own + depth + i] = far_speed[1, i]
            for lower in (True, False):
                halo_copy(lower).wait()
        side = start
        place_halo(halo_first if block == 0 else halo_next, width, side)
        for r in range(width - 1):
            if own - 2 - 2 * r >= 0:
                sweep_edges(side, r, width)
            else:
                total = own + 2 * (width - 1 - r)
                sweep(side, total, ghost - width + 1 + r, into(1 - side), True)
            side = 1 - side
        if block == 0:
            sweep(side, own, ghost, into_edge(1 - side))
            for lower in (True, False):
                halo_copy(lower).start()
            side = 1 - side
        else:
            sweep(side, own, ghost, into_stage)

    def block_copy(j):
        other = lax.rem(member + j, members)
        return pltpu.make_async_remote_copy(
            src_ref=stage.at[other],
            dst_ref=arrived.at[station],
            send_sem=all_send.at[j],
            recv_sem=all_recv.at[station],
            device_id=member_at(other),
            device_id_type=mesh_id,
        )

    def block_arrival(j):
        other = lax.rem(member + j, members)
        source = NEAR * (lax.rem(other, stas)) + lax.div(other, stas)
        return pltpu.make_async_remote_copy(
            src_ref=stage.at[other],
            dst_ref=arrived.at[source],
            send_sem=all_send.at[j],
            recv_sem=all_recv.at[source],
            device_id=member_at(other),
            device_id_type=mesh_id,
        )

    def start_block(j, carry):
        block_copy(j).start()
        return carry

    def end_block(j, carry):
        block_copy(j).wait_send()
        block_arrival(j).wait_recv()
        return carry

    lax.fori_loop(members // 4, members, start_block, 0)
    lax.fori_loop(1, members // 4, start_block, 0)
    arrived[station] = stage[member]
    for j in range(10):
        start_copy(j).wait_send()
    lax.fori_loop(1, members, end_block, 0)
    refined_ref[...] = arrived[...]


def refined_tables(coarse_times, model_map, slowness, picks, pick_mask):
    per_device, depth, rows, lanes = coarse_times.shape
    stas = lax.axis_size("sta")
    stations = per_device * stas
    near, ghost = BLOCKS
    own = NEAR * depth
    assert per_device == NEAR and sum(BLOCKS) == ROUNDS and near < depth < ghost <= own
    piece = rows // stas
    count = own + 2 * ghost
    plane = (rows, lanes)
    vmem = pl.BlockSpec(memory_space=pltpu.VMEM)
    dma = pltpu.SemaphoreType.DMA
    events = picks.shape[0]
    wide = (events, lanes)
    hbm = pl.BlockSpec(memory_space=pltpu.HBM)
    return pl.pallas_call(
        travel_kernel,
        out_shape=(
            jax.ShapeDtypeStruct((stations, depth, piece, lanes), jnp.float32),
            jax.ShapeDtypeStruct(wide, jnp.float32),
            jax.ShapeDtypeStruct((stations,) + wide, jnp.float32),
            jax.ShapeDtypeStruct((stations,) + wide, jnp.float32),
            jax.ShapeDtypeStruct(wide, jnp.float32),
            jax.ShapeDtypeStruct(wide, jnp.float32),
        ),
        in_specs=[hbm] * 5,
        out_specs=[vmem] * 6,
        scratch_shapes=[
            pltpu.VMEM(wide, jnp.float32),
            pltpu.VMEM((depth,) + plane, jnp.float32),
            pltpu.VMEM((depth,) + plane, jnp.int32),
            pltpu.SMEM(slowness.shape, jnp.float32),
            pltpu.VMEM((stations, events), jnp.float32),
            pltpu.VMEM((stations, events), jnp.int32),
            dma((5,)),
            pltpu.VMEM((depth,) + plane, jnp.float32),
            pltpu.VMEM((2, count, rows + 2 * PAD, lanes), jnp.float32),
            pltpu.VMEM((count,) + plane, jnp.float32),
            pltpu.VMEM((depth,) + plane, jnp.float32),
            pltpu.VMEM((depth,) + plane, jnp.float32),
            pltpu.VMEM((2, near) + plane, jnp.float32),
            pltpu.VMEM((2, ghost) + plane, jnp.float32),
            pltpu.VMEM((2, near) + plane, jnp.float32),
            pltpu.VMEM((2, depth - near) + plane, jnp.float32),
            pltpu.VMEM((2, ghost - depth) + plane, jnp.float32),
            pltpu.VMEM((own,) + plane, jnp.float32),
            pltpu.VMEM((NEAR * stas, depth, piece, lanes), jnp.float32),
            pltpu.VMEM((stations, depth, piece, lanes), jnp.float32),
            dma((10,)),
            dma((10,)),
            dma((2,)),
            dma((2,)),
            dma((NEAR * stas,)),
            dma((stations,)),
        ],
        compiler_params=pltpu.CompilerParams(collective_id=1, has_side_effects=True, vmem_limit_bytes=16 << 20),
        name="travel",
    )(*[pltpu.with_memory_space_constraint(x, pltpu.HBM) for x in (coarse_times, model_map, slowness, picks.T, pick_mask.T)])


def locate_kernel(
    times_ref,
    mask_rows,
    arrival_ref,
    seen_ref,
    mean_ref,
    share_ref,
    weight_ref,
    peak_ref,
    stats_ref,
    picked_sum,
    score,
    lane_mass,
    first,
    second,
    local,
    mid,
    send_sem,
    recv_sem,
):
    space = lax.axis_index("space")
    sta = lax.axis_index("sta")
    stas = lax.axis_size("sta")
    lines = lax.axis_size("space") // NEAR
    line = lax.div(space, NEAR)
    member = (lax.rem(space, NEAR)) * stas + sta
    members = NEAR * stas

    def member_id(k):
        other = lax.rem(member + k, members)
        return {"space": line * NEAR + lax.div(other, stas), "sta": lax.rem(other, stas)}

    def line_id(k):
        return {"space": lax.rem(line + k, lines) * NEAR + lax.rem(space, NEAR), "sta": sta}

    barrier = pltpu.get_barrier_semaphore()

    def greet(ids, count):
        def one(k, carry):
            pl.semaphore_signal(barrier, inc=1, device_id=ids(k), device_id_type=pl.DeviceIdType.MESH)
            return carry

        lax.fori_loop(1, count, one, 0)

    greet(member_id, members)
    greet(line_id, lines)

    rows, events, lanes = weight_ref.shape
    stations = times_ref.shape[0] // rows
    blocks = events // lanes

    chosen = mask_rows[...].astype(jnp.bfloat16)
    blank = jnp.zeros((lanes - 3 * stations, lanes), jnp.float32)

    def pieces(row):
        part = times_ref[pl.ds(row, stations, stride=rows)]
        high = part.astype(jnp.bfloat16).astype(jnp.float32)
        rest = part - high
        middle = rest.astype(jnp.bfloat16).astype(jnp.float32)
        return jnp.concatenate([high, middle, rest - middle, blank], 0).astype(jnp.bfloat16)

    def sums(pair, carry):
        right = jnp.concatenate([pieces(2 * pair), pieces(2 * pair + 1)], 1)
        both = jnp.dot(chosen, right, preferred_element_type=jnp.float32)
        picked_sum[2 * pair] = both[:, :lanes]
        picked_sum[2 * pair + 1] = both[:, lanes:]
        return carry

    lax.fori_loop(0, rows // 2, sums, 0)

    def tile(index, carry):
        cut = pl.ds(pl.multiple_of(index * EVENT_TILE, EVENT_TILE), EVENT_TILE)
        shape = (EVENT_TILE, lanes)
        arrival = [arrival_ref[s, cut] for s in range(stations)]
        seen = [seen_ref[s, cut] for s in range(stations)]
        mean = mean_ref[cut]
        share = share_ref[cut]

        def row(r, top):
            shift = mean - picked_sum[r, cut] * share
            sums = [None] * 4
            for s in range(stations):
                time = jnp.broadcast_to(times_ref[pl.ds(s * rows + r, 1)], shape)
                deviation = (arrival[s] - time) - shift
                term = seen[s] * (deviation * deviation)
                sums[s % 4] = term if sums[s % 4] is None else sums[s % 4] + term
            misfit = functools.reduce(jnp.add, [part for part in sums if part is not None])
            value = (-0.5 / (pick_sigma * pick_sigma)) * misfit
            score[r] = value
            return jnp.maximum(top, value)

        low = jnp.full(shape, -3.0e38, jnp.float32)
        top = lax.fori_loop(0, rows, row, low, unroll=ROW_UNROLL)
        mass = jnp.zeros(shape, jnp.float32)
        for r in range(rows):
            weight = jnp.exp(score[r] - top)
            weight_ref[r, cut] = weight
            mass = mass + weight
        peak_ref[cut] = top
        lane_mass[cut] = mass
        return carry

    lax.fori_loop(0, events // EVENT_TILE, tile, 0)

    for b in range(blocks):
        cut = pl.ds(b * lanes, lanes)
        peak = peak_ref[cut].T
        top = jnp.max(peak, 0, keepdims=True)
        mass = jnp.sum(lane_mass[cut].T * jnp.exp(peak - top), 0, keepdims=True)
        local[pl.ds(b, 1)] = top
        local[pl.ds(blocks + b, 1)] = mass

    pl.semaphore_wait(barrier, members + lines - 2)

    def exchange(src, slots, ids, count, phase):
        def copy(k):
            return pltpu.make_async_remote_copy(
                src_ref=src,
                dst_ref=slots.at[k - 1],
                send_sem=send_sem.at[phase, k - 1],
                recv_sem=recv_sem.at[phase, k - 1],
                device_id=ids(k),
                device_id_type=pl.DeviceIdType.MESH,
            )

        def start(k, carry):
            copy(k).start()
            return carry

        def wait(k, carry):
            copy(k).wait()
            return carry

        lax.fori_loop(count // 4, count, start, 0)
        lax.fori_loop(1, count // 4, start, 0)
        lax.fori_loop(1, count, wait, 0)

    def merged(top, mass, slots, count):
        best = top
        for k in range(count):
            best = jnp.maximum(best, slots[k, :blocks])
        total = mass * jnp.exp(top - best)
        for k in range(count):
            total = total + slots[k, blocks:] * jnp.exp(slots[k, :blocks] - best)
        return best, total

    exchange(local, first, member_id, members, 0)
    top, mass = merged(local[:blocks], local[blocks:], first, members - 1)
    mid[:blocks] = top
    mid[blocks:] = mass
    exchange(mid, second, line_id, lines, 1)
    top, mass = merged(top, mass, second, lines - 1)
    stats_ref[:blocks] = top
    stats_ref[blocks:] = mass


def density_kernel(
    weight_ref, peak_ref, stats_ref, refined_ref, out_ref, table_ref, scale, chunk, sem, table_sem
):
    table = pltpu.make_async_copy(refined_ref, table_ref, table_sem)
    table.start()
    rows, events, lanes = weight_ref.shape
    blocks = events // lanes
    size = chunk.shape[1] // rows
    for b in range(blocks):
        cut = pl.ds(b * lanes, lanes)
        top = jnp.broadcast_to(stats_ref[pl.ds(b, 1)], (lanes, lanes)).T
        mass = jnp.broadcast_to(stats_ref[pl.ds(blocks + b, 1)], (lanes, lanes)).T
        scale[cut] = jnp.exp(peak_ref[cut] - top) / mass

    def copy(c, slot):
        return pltpu.make_async_copy(
            chunk.at[slot], out_ref.at[pl.ds(c * size * rows, size * rows)], sem.at[slot]
        )

    slots = chunk.shape[0]
    chunks = events // size
    for c in range(chunks):
        slot = c % slots
        if c >= slots:
            copy(c - slots, slot).wait()
        for t in range(size // EVENT_TILE):
            cut = pl.ds(c * size + t * EVENT_TILE, EVENT_TILE)
            factor = scale[cut]
            for r in range(rows):
                chunk[slot, pl.ds(t * EVENT_TILE * rows + r, EVENT_TILE, stride=rows)] = (
                    weight_ref[r, cut] * factor
                )
        copy(c, slot).start()
    for c in range(chunks - slots, chunks):
        copy(c, c % slots).wait()
    table.wait()


def event_density(refined, mask_rows, *events_over_lanes):
    stations, depth, piece, lanes = refined.shape
    events = mask_rows.shape[0]
    rows = depth * piece
    assert 3 * stations <= lanes and events % lanes == 0 and rows % 2 == 0
    blocks = events // lanes
    members = NEAR * lax.axis_size("sta")
    lines = lax.axis_size("space") // NEAR
    longest = max(members, lines)
    vmem = pl.BlockSpec(memory_space=pltpu.VMEM)
    wide = (events, lanes)
    message = (2 * blocks, lanes)
    f32 = jnp.float32
    weight, peak, stats = pl.pallas_call(
        locate_kernel,
        out_shape=(
            jax.ShapeDtypeStruct((rows,) + wide, f32),
            jax.ShapeDtypeStruct(wide, f32),
            jax.ShapeDtypeStruct(message, f32),
        ),
        in_specs=[vmem] * 6,
        out_specs=[vmem] * 3,
        scratch_shapes=[
            pltpu.VMEM((rows,) + wide, f32),
            pltpu.VMEM((rows, EVENT_TILE, lanes), f32),
            pltpu.VMEM(wide, f32),
            pltpu.VMEM((members - 1,) + message, f32),
            pltpu.VMEM((lines - 1,) + message, f32),
            pltpu.VMEM(message, f32),
            pltpu.VMEM(message, f32),
            pltpu.SemaphoreType.DMA((2, longest)),
            pltpu.SemaphoreType.DMA((2, longest)),
        ],
        compiler_params=pltpu.CompilerParams(collective_id=0, has_side_effects=True, vmem_limit_bytes=16 << 20),
        name="locate",
    )(refined.reshape(stations * rows, lanes), mask_rows, *events_over_lanes)
    density, table = pl.pallas_call(
        density_kernel,
        out_shape=(
            jax.ShapeDtypeStruct((events * rows, lanes), f32),
            jax.ShapeDtypeStruct(refined.shape, f32),
        ),
        in_specs=[vmem] * 4,
        out_specs=[pl.BlockSpec(memory_space=pltpu.HBM)] * 2,
        scratch_shapes=[
            pltpu.VMEM(wide, f32),
            pltpu.VMEM((4, 32 * rows, lanes), f32),
            pltpu.SemaphoreType.DMA((4,)),
            pltpu.SemaphoreType.DMA,
        ],
        compiler_params=pltpu.CompilerParams(vmem_limit_bytes=16 << 20),
        name="density",
    )(weight, peak, stats, refined)
    return table, density.reshape(events, depth, piece, lanes)


def body(coarse_times, model_map, slowness, picks, pick_mask):
    refined, *events = refined_tables(coarse_times, model_map, slowness, picks, pick_mask)
    return event_density(refined, *events)


def solution(mesh):
    placed = (P("sta", "space", None, None), P("space", None, None), P(), P(), P())
    return jax.shard_map(
        body,
        mesh=mesh,
        in_specs=placed,
        out_specs=(P(None, "space", "sta", None), P(None, "space", "sta", None)),
        check_vma=False,
    )
```
